32 devices in a mesh: slab: 8 (over z, y), pencil: 4 (over x, core).
Axes of the slice: x: 2, y: 2, z: 4, core: 2. Of those that a mesh axis runs over, the one named last changes fastest.
Arguments:
- final_adjoint: bfloat16 [32, 128, 1024], P('slab', 'pencil'), may hold values from -6 to 6
- departure: int32 [4, 32, 128], P(None, 'slab', 'pencil'), may hold values from 1 to 29, as said below
- fraction: float32 [4, 32, 128, 1024], P(None, 'slab', 'pencil'), may hold values from 0 to 1
- image: float32 [32, 128, 1024], P('slab', 'pencil'), may hold values from -6 to 6
Outputs:
- adjoint_start: bfloat16 [32, 128, 1024], P('slab', 'pencil')
- body_force: float32 [3, 32, 128, 1024], P(None, 'slab', 'pencil')
The draws below stay inside these ranges and needn't reach their ends.
Inputs may be any that keep to these rules, and one draw needn't show every extreme that they name: Each base row departure[s][i, j] equals i + d, kept within the volume's range, with an integer displacement d of magnitude at most 4; in every step some blocks have d = 4 and some d = -4.
All inputs are finite; a program needn't handle non-finite values.
Results may differ from the reference program's by a relative error of at most 0.0055.
Values sent between devices are 32-bit elements; how exact they have to be, the bound alone decides.
A program may use at most 64 MiB of HBM per device.

```python
import jax
import jax.numpy as jnp

CX = 4
LINE = 1024
STEPS = 4
NX = 32
NY = 128


def draw_departure(key, part):
    rows = jnp.arange(NX, dtype=jnp.int32)[:, None]

    def one_step(step):
        step_key = jax.random.fold_in(key, step + 101)
        key_stripe, key_jitter, key_pick = jax.random.split(step_key, 3)
        stripe = jax.random.randint(key_stripe, (NY,), -2 * CX, 2 * CX + 1)
        picked = jax.random.permutation(key_pick, NY)
        stripe = stripe.at[picked[0]].set(2 * CX + 1)
        stripe = stripe.at[picked[1]].set(-2 * CX - 1)
        jitter = jax.random.randint(key_jitter, (NX, NY), -1, 2)
        moved = jnp.clip(stripe[None, :] + jitter, -CX, CX)
        return jnp.clip(rows + moved, 1, NX - 3).astype(jnp.int32)
    return jnp.stack([one_step(step) for step in range(STEPS)], axis=0)


def steps_of(rng, dims, shards, least, top_value):
    gain, own = 1.0, jax.random.fold_in(rng, 6)
    for position, parts in shards:
        steps = jnp.exp(jax.random.uniform(jax.random.fold_in(own, position), (parts,), jnp.float32, least / len(shards), top_value / len(shards)))
        gain = gain * jnp.repeat(steps, dims[position] // parts).reshape([-1 if axis == position else 1 for axis in range(len(dims))])
    return gain


def centred(own_key, shape, scale, reach, cuts=(), kind=jnp.bfloat16):
    values = scale * jax.random.normal(own_key, shape, jnp.float32)
    if cuts:
        values = values * steps_of(own_key, shape, cuts, -0.22, 0.18)
    return jnp.clip(values, -reach, reach).astype(kind)


def setup_inputs(seed: int = 0) -> dict:
    key_of = jax.random.split(jax.random.key(seed), 5)
    return {
        "final_adjoint": centred(key_of[0], (NX, NY, LINE), 1.0, 6.0, ((0, 8), (1, 4))),
        "departure": draw_departure(jax.random.fold_in(key_of[4], 71), 0),
        "fraction": jnp.clip(1.0 * jax.random.uniform(key_of[2], (STEPS, NX, NY, LINE), jnp.float32) ** steps_of(key_of[2], (STEPS, NX, NY, LINE), ((1, 8), (2, 4)), -0.2, 0.2), 0.0, 1.0),
        "image": centred(key_of[3], (NX, NY, LINE), 1.0, 6.0, ((0, 8), (1, 4)), jnp.float32),
    }


def spline_weights(fraction):
    rest = 1.0 - fraction
    square = fraction * fraction
    cube = square * fraction
    return (rest * rest * rest / 6.0,
            (3.0 * cube - 6.0 * square + 4.0) / 6.0,
            (-3.0 * cube + 3.0 * square + 3.0 * fraction + 1.0) / 6.0,
            cube / 6.0)


def reference(final_adjoint, departure, fraction, image):
    adjoint = final_adjoint
    column_index = jnp.broadcast_to(jnp.arange(NY, dtype=jnp.int32)[None, :], (NX, NY))
    for step in reversed(range(STEPS)):
        values = adjoint.astype(jnp.float32)
        weights = spline_weights(fraction[step])
        splat = jnp.zeros((NX, NY, LINE), jnp.float32)
        for offset in range(4):
            landing = (departure[step] + (offset - 1)).astype(jnp.int32)
            splat = splat.at[landing, column_index].add(weights[offset] * values)
        adjoint = splat.astype(jnp.bfloat16)
    padded = jnp.pad(image, 1)
    along_first = (padded[2:, 1:-1, 1:-1] - padded[:-2, 1:-1, 1:-1]) * 0.5
    along_second = (padded[1:-1, 2:, 1:-1] - padded[1:-1, :-2, 1:-1]) * 0.5
    along_third = (padded[1:-1, 1:-1, 2:] - padded[1:-1, 1:-1, :-2]) * 0.5
    weight_field = adjoint.astype(jnp.float32)
    body_force = jnp.stack([weight_field * along_first, weight_field * along_second, weight_field * along_third], axis=0)
    return adjoint, body_force
```

```python
import functools

import jax
import jax.numpy as jnp
from jax import lax
from jax.experimental import pallas as pl
from jax.experimental.pallas import tpu as pltpu
from jax.sharding import PartitionSpec as P

BELOW = 5
ABOVE = 6
TILE = 8
WIDTH = 256
LAG = 6
AHEAD = 12
IMAGE_SLOT = 4
IMAGE_GAP = 3
MESH = pl.DeviceIdType.MESH


def kernel(
    slabs,
    pencils,
    dep_ref,
    adj_ref,
    frac_ref,
    img_ref,
    adj_out,
    grad_out,
    dep_buf,
    land_buf,
    adj_buf,
    stage,
    cur,
    frac_own,
    frac_rx,
    acc,
    tx_up,
    tx_dn,
    rx_lo,
    rx_hi,
    img_pad,
    relay_buf,
    dep_sem,
    own_dep_sem,
    adj_sem,
    cur_send,
    cur_recv,
    own_sem,
    frac_send,
    frac_recv,
    up_send,
    up_recv,
    dn_send,
    dn_recv,
    back_send,
    back_recv,
    img_sem,
    halo_sem,
    inner_sem,
    outer_sem,
):
    s = lax.axis_index("slab")
    p = lax.axis_index("pencil")
    y = lax.rem(s, 2)
    other = 1 - y
    partner = s + 1 - 2 * y
    pair = lax.div(s, 2)
    has_lower = s >= 2
    has_upper = s + 2 < slabs

    rows, cols, line = adj_out.shape
    half = line // 2
    width = stage.shape[-1]
    parts = half // width
    tiles = cols // TILE
    chunks = tiles * parts
    steps = frac_ref.shape[0]
    tall = 2 * rows
    span = BELOW + tall + ABOVE
    slots = chunks + steps * LAG

    def remote(src, dst, send_sem, recv_sem, where):
        return pltpu.make_async_remote_copy(
            src_ref=src,
            dst_ref=dst,
            send_sem=send_sem,
            recv_sem=recv_sem,
            device_id=where,
            device_id_type=MESH,
        )

    def place(c, start):
        first = pl.multiple_of(lax.div(c, parts) * TILE, TILE)
        lanes = pl.multiple_of(start + lax.rem(c, parts) * width, width)
        return pl.ds(first, TILE), pl.ds(lanes, width)

    def own_copy(u):
        return pltpu.make_async_copy(
            frac_ref.at[steps - 1 - u, :, :, pl.ds(pl.multiple_of(y * half, half), half)],
            frac_own.at[u],
            own_sem.at[u],
        )

    def frac_copy(u, c):
        return remote(
            frac_ref.at[(steps - 1 - u, slice(None)) + place(c, other * half)],
            frac_rx.at[(u, slice(None)) + place(c, 0)],
            frac_send,
            frac_recv.at[u, c],
            {"slab": partner},
        )

    def cur_copy(c):
        return remote(stage.at[1, c], cur.at[c], cur_send, cur_recv.at[c], {"slab": partner})

    def dep_copy_to(slot):
        return remote(dep_ref, dep_buf.at[slot], dep_sem.at[0], dep_sem.at[1], {"slab": partner})

    def up_copy(u, c):
        return remote(tx_up.at[u, c], rx_lo.at[u, c], up_send, up_recv.at[u, c], {"slab": s + 2})

    def dn_copy(u, c):
        return remote(tx_dn.at[u, c], rx_hi.at[u, c], dn_send, dn_recv.at[u, c], {"slab": s - 2})

    def back_copy(c):
        return remote(
            acc.at[c, pl.ds(other * rows, rows)],
            adj_out.at[(slice(None),) + place(c, y * half)],
            back_send,
            back_recv,
            {"slab": partner},
        )

    center_cols = pl.ds(TILE, cols)
    image_copy = pltpu.make_async_copy(
        img_ref, img_pad.at[pl.ds(1, rows), center_cols], img_sem
    )
    relay_to = s + 4 * y - 2
    relay_from = s + 2 - 4 * y
    outer = s + 2 * y - 1
    sends_relay = jnp.logical_and(relay_to >= 0, relay_to < slabs)
    gets_relay = jnp.logical_and(relay_from >= 0, relay_from < slabs)
    gets_outer = jnp.logical_and(outer >= 0, outer < slabs)

    def halo(src, dst, index, where):
        return remote(src, dst, halo_sem.at[0, index], halo_sem.at[1, index], where)

    relay_copy = halo(img_ref.at[pl.ds(y * (rows - 1), 1)], relay_buf, 0, {"slab": relay_to})

    def edge_copy(row, src, src_row, sems, q):
        first = pl.multiple_of(q * TILE, TILE)
        return remote(
            src.at[pl.ds(src_row, 1), pl.ds(first, TILE)],
            img_pad.at[pl.ds(row, 1), pl.ds(pl.multiple_of(first + TILE, TILE), TILE)],
            sems.at[0, q],
            sems.at[1, q],
            {"slab": partner},
        )

    def outer_copy(q):
        return edge_copy(other * (rows + 1), relay_buf, 0, outer_sem, q)

    def inner_copy(q):
        return edge_copy(y * (rows + 1), img_ref, other * (rows - 1), inner_sem, q)

    halos = (
        (p + 1 < pencils, p >= 1, halo(
            img_ref.at[:, pl.ds(cols - TILE, TILE)], img_pad.at[pl.ds(1, rows), pl.ds(0, TILE)],
            1, {"pencil": p + 1})),
        (p >= 1, p + 1 < pencils, halo(
            img_ref.at[:, pl.ds(0, TILE)], img_pad.at[pl.ds(1, rows), pl.ds(cols + TILE, TILE)],
            2, {"pencil": p - 1})),
    )

    barrier = pltpu.get_barrier_semaphore()
    for there, where in (
        (slabs > 1, {"slab": partner}),
        (has_lower, {"slab": s - 2}),
        (has_upper, {"slab": s + 2}),
        (p >= 1, {"pencil": p - 1}),
        (p + 1 < pencils, {"pencil": p + 1}),
    ):
        @pl.when(there)
        def _():
            pl.semaphore_signal(barrier, inc=1, device_id=where, device_id_type=MESH)

    adj_copy = pltpu.make_async_copy(adj_ref, adj_buf, adj_sem)
    dep_copy = pltpu.make_async_copy(dep_ref, dep_buf.at[y], own_dep_sem)
    dep_copy.start()
    adj_copy.start()
    for u in range(steps):
        own_copy(u).start()
    image_copy.start()

    lane = lax.broadcasted_iota(jnp.int32, (steps, 4 * rows * TILE), 1)
    lane_row = lax.rem(lax.div(lane, TILE), rows)
    fixed = lane_row + lax.div(lane, rows * TILE) - 1 + BELOW
    fixed = fixed * TILE + lax.rem(lane, TILE)
    pick_lane = lax.broadcasted_iota(jnp.int32, (cols, 4 * rows * TILE), 1)
    pick_col = lax.broadcasted_iota(jnp.int32, (cols, 4 * rows * TILE), 0)
    keep_lane = lax.broadcasted_iota(jnp.int32, (steps * rows, 4 * rows * TILE), 1)
    keep_row = lax.broadcasted_iota(jnp.int32, (steps * rows, 4 * rows * TILE), 0)
    keep = lax.rem(keep_row, rows) == lax.rem(lax.div(keep_lane, TILE), rows)
    group_step = lax.broadcasted_iota(jnp.int32, (steps, steps * rows), 0)
    group_row = lax.broadcasted_iota(jnp.int32, (steps, steps * rows), 1)
    group = jnp.where(group_step == lax.div(group_row, rows), 1.0, 0.0).astype(jnp.bfloat16)
    row_of = lax.broadcasted_iota(jnp.int32, (rows, cols), 0)

    def landing(h):
        first_row = pair * tall + h * rows
        moved = jnp.concatenate([dep_buf[h, k] - row_of - first_row for k in range(steps)], axis=0)
        moved = moved.astype(jnp.float32).astype(jnp.bfloat16)
        for tile in range(tiles):
            pick = pick_col == tile * TILE + lax.rem(pick_lane, TILE)
            pick = jnp.where(pick, 1.0, 0.0).astype(jnp.bfloat16)
            spread = jnp.dot(moved, pick, preferred_element_type=jnp.float32)
            spread = jnp.where(keep, spread, 0.0).astype(jnp.bfloat16)
            by_step = jnp.dot(group, spread, preferred_element_type=jnp.float32)
            land_buf[h, tile] = fixed + h * rows * TILE + by_step.astype(jnp.int32) * TILE

    adj_copy.wait()
    for q in range(cols // (2 * TILE)):
        for h in range(2):
            for k in range(parts):
                lanes = pl.ds(pl.multiple_of((y if h == 0 else other) * half + width * k, width), width)
                wide = adj_buf[:, 2 * TILE * q : 2 * TILE * (q + 1), lanes].astype(jnp.float32)
                stage[h, 2 * q * parts + k] = wide[:, :TILE]
                stage[h, (2 * q + 1) * parts + k] = wide[:, TILE:]
    dep_copy.wait()
    landing(y)

    peers = sum(
        jnp.where(there, 1, 0)
        for there in (slabs > 1, has_lower, has_upper, p >= 1, p + 1 < pencils)
    )
    pl.semaphore_wait(barrier, peers)

    def feed(k):
        def later(i, z):
            u = steps - 1 - i
            c = k - u * LAG

            @pl.when(jnp.logical_and(c >= 0, c < chunks))
            def _():
                frac_copy(u, c).start()

            return z

        lax.fori_loop(0, steps - 1, later, 0)

        @pl.when(k < chunks)
        def _():
            cur_copy(k).start()
            frac_copy(0, k).start()

    dep_copy_to(y).start()
    feed(jnp.int32(0))

    @pl.when(sends_relay)
    def _():
        relay_copy.start()

    lax.fori_loop(1, AHEAD, lambda k, z: (feed(k), z)[1], 0)
    for send, _, copy in halos:
        @pl.when(send)
        def _():
            copy.start()

    dep_copy_to(other).wait_recv()
    landing(other)

    target = lax.broadcasted_iota(jnp.int32, (span * TILE, 4 * rows * TILE), 0)

    def splat(u, c, mine, theirs):
        frac_copy(u, c).wait_recv()
        weighted = []
        hots = []
        tile = lax.div(c, parts)
        for h, held, v in ((y, frac_own, mine), (other, frac_rx, theirs)):
            f = held[(u, slice(None)) + place(c, 0)].reshape(rows * TILE, width)
            v = v.reshape(rows * TILE, width)
            rest = 1.0 - f
            square = f * f
            cube = square * f
            sixth = v * (1.0 / 6.0)
            weighted.append(rest * rest * rest * sixth)
            weighted.append((3.0 * cube - 6.0 * square + 4.0) * sixth)
            weighted.append((-3.0 * cube + 3.0 * square + 3.0 * f + 1.0) * sixth)
            weighted.append(cube * sixth)
            land = land_buf[h, tile, pl.ds(steps - 1 - u, 1), :]
            hots.append(jnp.where(target == land, 1.0, 0.0).astype(jnp.bfloat16))
        hot = jnp.concatenate(hots, axis=1)
        high = [part.astype(jnp.bfloat16) for part in weighted]
        low = [(a - b.astype(jnp.float32)).astype(jnp.bfloat16) for a, b in zip(weighted, high)]
        both = jnp.concatenate([jnp.concatenate(high, axis=0), jnp.concatenate(low, axis=0)], axis=1)
        out = jnp.dot(hot, both, preferred_element_type=jnp.float32)
        out = (out[:, :width] + out[:, width:]).reshape(span, TILE, width)
        tx_dn[u, c] = out[:BELOW]
        tx_up[u, c] = out[BELOW + tall :]

        @pl.when(has_upper)
        def _():
            up_copy(u, c).start()

        @pl.when(has_lower)
        def _():
            dn_copy(u, c).start()

        acc[c] = out[BELOW : BELOW + tall]

    def combine(u, c):
        @pl.when(has_lower)
        def _():
            up_copy(u, c).wait_recv()
            acc[c, :ABOVE] += rx_lo[u, c]

        @pl.when(has_upper)
        def _():
            dn_copy(u, c).wait_recv()
            acc[c, tall - BELOW :] += rx_hi[u, c]

    def rounded(c, h):
        return acc[c, pl.ds(h * rows, rows)].astype(jnp.bfloat16).astype(jnp.float32)

    grad_lane = lax.broadcasted_iota(jnp.int32, (cols, line), 1)

    def gradient(r):
        grad_out[0, r] = (img_pad[r + 2, TILE : TILE + cols] - img_pad[r, TILE : TILE + cols]) * 0.5
        grad_out[1, r] = (
            img_pad[r + 1, TILE + 1 : TILE + cols + 1] - img_pad[r + 1, TILE - 1 : TILE + cols - 1]
        ) * 0.5
        center = img_pad[r + 1, TILE : TILE + cols]
        after = jnp.where(grad_lane == line - 1, 0.0, pltpu.roll(center, line - 1, 1))
        before = jnp.where(grad_lane == 0, 0.0, pltpu.roll(center, 1, 1))
        grad_out[2, r] = (after - before) * 0.5

    def slot(k, z):
        feed(k + AHEAD)

        since = k - IMAGE_SLOT
        q = lax.div(since, IMAGE_GAP)
        turn = jnp.logical_and(since >= 0, lax.rem(since, IMAGE_GAP) == 0)

        @pl.when(jnp.logical_and(turn, q < tiles))
        def _():
            inner_copy(q).start()

            @pl.when(jnp.logical_and(gets_relay, q == 0))
            def _():
                relay_copy.wait_recv()

            @pl.when(gets_relay)
            def _():
                outer_copy(q).start()

        last = k - steps * LAG

        @pl.when(last >= 0)
        def _():
            combine(steps - 1, last)
            acc[last, pl.ds(other * rows, rows)] = rounded(last, other)
            back_copy(last).start()
            adj_out[(slice(None),) + place(last, y * half)] = rounded(last, y)

        def later(i, z):
            u = steps - 1 - i
            c = k - u * LAG

            @pl.when(jnp.logical_and(c >= 0, c < chunks))
            def _():
                combine(u - 1, c)
                splat(u, c, rounded(c, y), rounded(c, other))

            return z

        lax.fori_loop(0, steps - 1, later, 0)

        @pl.when(k < chunks)
        def _():
            cur_copy(k).wait_recv()

            @pl.when(k == 0)
            def _():
                for u in range(steps):
                    own_copy(u).wait()

            splat(0, k, stage[0, k], cur[k])

        @pl.when(k == slots - LAG)
        def _():
            image_copy.wait()
            for q in range(tiles):
                inner_copy(q).wait_recv()

                @pl.when(gets_outer)
                def _():
                    outer_copy(q).wait_recv()

            @pl.when(jnp.logical_not(gets_outer))
            def _():
                img_pad[y * (rows + 1), TILE : TILE + cols] = jnp.zeros((cols, line), jnp.float32)

            for index, (_, receive, copy) in enumerate(halos):
                edge = 0 if index == 0 else cols + TILE

                @pl.when(receive)
                def _():
                    copy.wait_recv()

                @pl.when(jnp.logical_not(receive))
                def _():
                    img_pad[1 : rows + 1, edge : edge + TILE] = jnp.zeros((rows, TILE, line), jnp.float32)

            lax.fori_loop(0, rows, lambda r, z: (gradient(r), z)[1], 0)

        return z

    lax.fori_loop(0, slots, slot, 0)

    mine_half = pl.ds(pl.multiple_of(y * half, half), half)
    other_half = pl.ds(pl.multiple_of(other * half, half), half)
    dep_copy_to(y).wait_send()
    remote(stage.at[1], cur, cur_send, cur_recv.at[0], {"slab": partner}).wait_send()
    remote(
        frac_ref.at[:, :, :, other_half], frac_rx, frac_send, frac_recv.at[0, 0], {"slab": partner}
    ).wait_send()

    @pl.when(has_upper)
    def _():
        remote(tx_up, rx_lo, up_send, up_recv.at[0, 0], {"slab": s + 2}).wait_send()

    @pl.when(has_lower)
    def _():
        remote(tx_dn, rx_hi, dn_send, dn_recv.at[0, 0], {"slab": s - 2}).wait_send()

    for q in range(tiles):
        inner_copy(q).wait_send()

        @pl.when(gets_relay)
        def _():
            outer_copy(q).wait_send()

    @pl.when(sends_relay)
    def _():
        relay_copy.wait_send()

    for send, _, copy in halos:
        @pl.when(send)
        def _():
            copy.wait_send()

    back_all = remote(
        adj_out.at[:, :, mine_half], adj_out.at[:, :, other_half], back_send, back_recv, {"slab": partner}
    )
    back_all.wait_recv()
    back_all.wait_send()


def forces(adj_ref, grad_ref, adj_out, force_out, adj_buf, force_buf, adj_sem, force_sem):
    copies = []
    for r in range(adj_ref.shape[0]):
        mine = adj_ref[r]
        for c in range(3):
            force_buf[c, r] = mine * grad_ref[c, r]
        copies.append(pltpu.make_async_copy(force_buf.at[:, r], force_out.at[:, r], force_sem.at[r]))
        copies[-1].start()
        adj_buf[r] = mine.astype(jnp.bfloat16)
        copies.append(pltpu.make_async_copy(adj_buf.at[r], adj_out.at[r], adj_sem.at[r]))
        copies[-1].start()
    for copy in copies:
        copy.wait()


def shards(slabs, pencils, final_adjoint, departure, fraction, image):
    steps, rows, cols = departure.shape
    line = image.shape[2]
    half = line // 2
    width = WIDTH if half % WIDTH == 0 else half
    tiles = cols // TILE
    chunks = tiles * (half // width)
    tall = 2 * rows
    assert slabs % 2 == 0 and ABOVE <= tall and cols % (2 * TILE) == 0 and half % 128 == 0

    f32 = jnp.float32
    dma = pltpu.SemaphoreType.DMA
    vmem = pl.BlockSpec(memory_space=pltpu.VMEM)
    hbm = pl.BlockSpec(memory_space=pltpu.HBM)
    adjoint, gradient = pl.pallas_call(
        functools.partial(kernel, slabs, pencils),
        name="splat",
        out_shape=(
            jax.ShapeDtypeStruct((rows, cols, line), f32),
            jax.ShapeDtypeStruct((3, rows, cols, line), f32),
        ),
        in_specs=[hbm, hbm, hbm, hbm],
        out_specs=(vmem, vmem),
        scratch_shapes=[
            pltpu.VMEM((2, steps, rows, cols), jnp.int32),
            pltpu.VMEM((2, tiles, steps, 4 * rows * TILE), jnp.int32),
            pltpu.VMEM((rows, cols, line), jnp.bfloat16),
            pltpu.VMEM((2, chunks, rows, TILE, width), f32),
            pltpu.VMEM((chunks, rows, TILE, width), f32),
            pltpu.VMEM((steps, rows, cols, half), f32),
            pltpu.VMEM((steps, rows, cols, half), f32),
            pltpu.VMEM((chunks, tall, TILE, width), f32),
            pltpu.VMEM((steps, chunks, ABOVE, TILE, width), f32),
            pltpu.VMEM((steps, chunks, BELOW, TILE, width), f32),
            pltpu.VMEM((steps, chunks, ABOVE, TILE, width), f32),
            pltpu.VMEM((steps, chunks, BELOW, TILE, width), f32),
            pltpu.VMEM((rows + 2, cols + 2 * TILE, line), f32),
            pltpu.VMEM((1, cols, line), f32),
            dma((2,)),
            dma(()),
            dma(()),
            dma(()),
            dma((chunks,)),
            dma((steps,)),
            dma(()),
            dma((steps, chunks)),
            dma(()),
            dma((steps, chunks)),
            dma(()),
            dma((steps, chunks)),
            dma(()),
            dma(()),
            dma(()),
            dma((2, 3)),
            dma((2, tiles)),
            dma((2, tiles)),
        ],
        compiler_params=pltpu.CompilerParams(
            collective_id=0, has_side_effects=True, vmem_limit_bytes=40 * 1024 * 1024
        ),
    )(*(pltpu.with_memory_space_constraint(a, pltpu.HBM) for a in (departure, final_adjoint, fraction, image)))
    return pl.pallas_call(
        forces,
        name="forces",
        out_shape=(
            jax.ShapeDtypeStruct((rows, cols, line), jnp.bfloat16),
            jax.ShapeDtypeStruct((3, rows, cols, line), f32),
        ),
        in_specs=[vmem, vmem],
        out_specs=(hbm, hbm),
        scratch_shapes=[
            pltpu.VMEM((rows, cols, line), jnp.bfloat16),
            pltpu.VMEM((3, rows, cols, line), f32),
            dma((rows,)),
            dma((rows,)),
        ],
        compiler_params=pltpu.CompilerParams(vmem_limit_bytes=16 * 1024 * 1024),
    )(adjoint, gradient)


def solution(mesh):
    in_specs = (
        P("slab", "pencil", None),
        P(None, "slab", "pencil"),
        P(None, "slab", "pencil", None),
        P("slab", "pencil", None),
    )
    out_specs = (P("slab", "pencil", None), P(None, "slab", "pencil", None))
    body = functools.partial(shards, mesh.shape["slab"], mesh.shape["pencil"])
    return jax.shard_map(body, mesh=mesh, in_specs=in_specs, out_specs=out_specs, check_vma=False)
```

```python
import functools

import jax
import jax.numpy as jnp
from jax import lax
from jax.experimental import pallas as pl
from jax.experimental.pallas import tpu as pltpu
from jax.sharding import PartitionSpec as P

BELOW = 5
ABOVE = 6
TILE = 8
WIDTH = 256
OFFSETS = (0, 4, 10, 16, 22)
AHEAD = 12
IMAGE_SLOT = 12
IMAGE_GAP = 1
SPLIT = True
MESH = pl.DeviceIdType.MESH


def kernel(
    slabs,
    pencils,
    dep_ref,
    adj_ref,
    frac_ref,
    img_ref,
    adj_out,
    grad_out,
    dep_buf,
    land_buf,
    adj_buf,
    stage,
    cur,
    frac_buf,
    hot_buf,
    acc,
    tx_up,
    tx_dn,
    rx_lo,
    rx_hi,
    img_pad,
    relay_buf,
    dep_sem,
    land_sem,
    adj_sem,
    cur_send,
    cur_recv,
    own_sem,
    frac_send,
    frac_recv,
    up_send,
    up_recv,
    dn_send,
    dn_recv,
    back_send,
    back_recv,
    img_sem,
    halo_sem,
    inner_sem,
    outer_sem,
):
    s = lax.axis_index("slab")
    p = lax.axis_index("pencil")
    y = lax.rem(s, 2)
    other = 1 - y
    partner = s + 1 - 2 * y
    pair = lax.div(s, 2)
    has_lower = s >= 2
    has_upper = s + 2 < slabs

    rows, cols, line = adj_out.shape
    half = line // 2
    width = stage.shape[-1]
    hot_rows = hot_buf.shape[2]
    parts = half // width
    tiles = cols // TILE
    chunks = tiles * parts
    steps = frac_ref.shape[0]
    tall = 2 * rows
    span = BELOW + tall + ABOVE
    offsets = OFFSETS if steps == 4 and chunks == 8 else tuple(u * chunks for u in range(steps + 1))
    last_slot = chunks - 1 + offsets[steps - 1]
    whole = ((0, 0, width),)
    split = ((0, 0, width // 2), (1, width // 2, width // 2)) if SPLIT and width % 256 == 0 else whole

    def remote(src, dst, send_sem, recv_sem, where):
        return pltpu.make_async_remote_copy(
            src_ref=src,
            dst_ref=dst,
            send_sem=send_sem,
            recv_sem=recv_sem,
            device_id=where,
            device_id_type=MESH,
        )

    def place(c, start, piece=whole[0]):
        _, skip, wide = piece
        first = pl.multiple_of(lax.div(c, parts) * TILE, TILE)
        lanes = pl.multiple_of(start + lax.rem(c, parts) * width + skip, wide)
        return pl.ds(first, TILE), pl.ds(lanes, wide)

    def cut(ref, at, piece):
        return ref.at[at + (slice(None), slice(None), pl.ds(piece[1], piece[2]))]

    def own_copy(u):
        return pltpu.make_async_copy(
            frac_ref.at[steps - 1 - u, :, :, pl.ds(pl.multiple_of(y * half, half), half)],
            frac_buf.at[y, u],
            own_sem.at[u],
        )

    def frac_copy(u, c, piece=whole[0]):
        return remote(
            frac_ref.at[(steps - 1 - u, slice(None)) + place(c, other * half, piece)],
            frac_buf.at[(y, u, slice(None)) + place(c, 0, piece)],
            frac_send,
            frac_recv.at[u, c, piece[0]],
            {"slab": partner},
        )

    def cur_copy(c, piece=whole[0]):
        return remote(
            cut(stage, (c,), piece), cut(cur, (y, c), piece), cur_send, cur_recv.at[c, piece[0]], {"slab": partner}
        )

    def land_copy(h):
        return remote(land_buf.at[h], land_buf.at[h], land_sem.at[0], land_sem.at[1], {"slab": partner})

    def up_copy(u, c, piece=whole[0]):
        return remote(
            cut(tx_up, (u, c), piece), cut(rx_lo, (u, c), piece), up_send, up_recv.at[u, c, piece[0]], {"slab": s + 2}
        )

    def dn_copy(u, c, piece=whole[0]):
        return remote(
            cut(tx_dn, (u, c), piece), cut(rx_hi, (u, c), piece), dn_send, dn_recv.at[u, c, piece[0]], {"slab": s - 2}
        )

    def back_copy(c, piece=whole[0]):
        return remote(
            acc.at[c, pl.ds(other * rows, rows), :, pl.ds(piece[1], piece[2])],
            adj_out.at[(slice(None),) + place(c, y * half, piece)],
            back_send,
            back_recv,
            {"slab": partner},
        )

    center_cols = pl.ds(TILE, cols)
    image_copy = pltpu.make_async_copy(
        img_ref, img_pad.at[pl.ds(1, rows), center_cols], img_sem
    )
    relay_to = s + 4 * y - 2
    relay_from = s + 2 - 4 * y
    outer = s + 2 * y - 1
    sends_relay = jnp.logical_and(relay_to >= 0, relay_to < slabs)
    gets_relay = jnp.logical_and(relay_from >= 0, relay_from < slabs)
    gets_outer = jnp.logical_and(outer >= 0, outer < slabs)

    def halo(src, dst, index, where):
        return remote(src, dst, halo_sem.at[0, index], halo_sem.at[1, index], where)

    relay_copy = halo(img_ref.at[pl.ds(y * (rows - 1), 1)], relay_buf, 0, {"slab": relay_to})

    def edge_copy(row, src, src_row, sems, q):
        first = pl.multiple_of(q * TILE, TILE)
        return remote(
            src.at[pl.ds(src_row, 1), pl.ds(first, TILE)],
            img_pad.at[pl.ds(row, 1), pl.ds(pl.multiple_of(first + TILE, TILE), TILE)],
            sems.at[0, q],
            sems.at[1, q],
            {"slab": partner},
        )

    def outer_copy(q):
        return edge_copy(other * (rows + 1), relay_buf, 0, outer_sem, q)

    def inner_copy(q):
        return edge_copy(y * (rows + 1), img_ref, other * (rows - 1), inner_sem, q)

    halos = (
        (p + 1 < pencils, p >= 1, halo(
            img_ref.at[:, pl.ds(cols - TILE, TILE)], img_pad.at[pl.ds(1, rows), pl.ds(0, TILE)],
            1, {"pencil": p + 1})),
        (p >= 1, p + 1 < pencils, halo(
            img_ref.at[:, pl.ds(0, TILE)], img_pad.at[pl.ds(1, rows), pl.ds(cols + TILE, TILE)],
            2, {"pencil": p - 1})),
    )

    barrier = pltpu.get_barrier_semaphore()
    for there, where in (
        (slabs > 1, {"slab": partner}),
        (has_lower, {"slab": s - 2}),
        (has_upper, {"slab": s + 2}),
        (p >= 1, {"pencil": p - 1}),
        (p + 1 < pencils, {"pencil": p + 1}),
    ):
        @pl.when(there)
        def _():
            pl.semaphore_signal(barrier, inc=1, device_id=where, device_id_type=MESH)

    adj_copy = pltpu.make_async_copy(adj_ref, adj_buf, adj_sem)
    dep_copy = pltpu.make_async_copy(dep_ref, dep_buf, dep_sem)
    dep_copy.start()
    adj_copy.start()
    for u in range(steps):
        own_copy(u).start()
    image_copy.start()

    lane = lax.broadcasted_iota(jnp.int32, (steps, 4 * rows * TILE), 1)
    lane_row = lax.rem(lax.div(lane, TILE), rows)
    fixed = lane_row + lax.div(lane, rows * TILE) - 1 + BELOW
    fixed = fixed * TILE + lax.rem(lane, TILE)
    pick_lane = lax.broadcasted_iota(jnp.int32, (cols, 4 * rows * TILE), 1)
    pick_col = lax.broadcasted_iota(jnp.int32, (cols, 4 * rows * TILE), 0)
    keep_lane = lax.broadcasted_iota(jnp.int32, (steps * rows, 4 * rows * TILE), 1)
    keep_row = lax.broadcasted_iota(jnp.int32, (steps * rows, 4 * rows * TILE), 0)
    keep = lax.rem(keep_row, rows) == lax.rem(lax.div(keep_lane, TILE), rows)
    group_step = lax.broadcasted_iota(jnp.int32, (steps, steps * rows), 0)
    group_row = lax.broadcasted_iota(jnp.int32, (steps, steps * rows), 1)
    group = jnp.where(group_step == lax.div(group_row, rows), 1.0, 0.0).astype(jnp.bfloat16)
    row_of = lax.broadcasted_iota(jnp.int32, (rows, cols), 0)

    def landing(h):
        first_row = pair * tall + h * rows
        moved = jnp.concatenate([dep_buf[k] - row_of - first_row for k in range(steps)], axis=0)
        moved = moved.astype(jnp.float32).astype(jnp.bfloat16)
        for tile in range(tiles):
            pick = pick_col == tile * TILE + lax.rem(pick_lane, TILE)
            pick = jnp.where(pick, 1.0, 0.0).astype(jnp.bfloat16)
            spread = jnp.dot(moved, pick, preferred_element_type=jnp.float32)
            spread = jnp.where(keep, spread, 0.0).astype(jnp.bfloat16)
            by_step = jnp.dot(group, spread, preferred_element_type=jnp.float32)
            land_buf[h, tile] = fixed + h * rows * TILE + by_step.astype(jnp.int32) * TILE

    adj_copy.wait()
    for q in range(cols // (2 * TILE)):
        for h in range(2):
            for k in range(parts):
                lanes = pl.ds(pl.multiple_of((y if h == 0 else other) * half + width * k, width), width)
                wide = adj_buf[:, 2 * TILE * q : 2 * TILE * (q + 1), lanes].astype(jnp.float32)
                if h == 0:
                    cur[y, 2 * q * parts + k] = wide[:, :TILE]
                    cur[y, (2 * q + 1) * parts + k] = wide[:, TILE:]
                else:
                    stage[2 * q * parts + k] = wide[:, :TILE]
                    stage[(2 * q + 1) * parts + k] = wide[:, TILE:]
    dep_copy.wait()
    landing(y)

    @pl.when(jnp.logical_not(has_lower))
    def _():
        rx_lo[...] = jnp.zeros_like(rx_lo)

    @pl.when(jnp.logical_not(has_upper))
    def _():
        rx_hi[...] = jnp.zeros_like(rx_hi)


    peers = sum(
        jnp.where(there, 1, 0)
        for there in (slabs > 1, has_lower, has_upper, p >= 1, p + 1 < pencils)
    )
    pl.semaphore_wait(barrier, peers)

    def feed(k):
        for u in range(steps - 1, 0, -1):
            c = k - offsets[u]

            @pl.when(jnp.logical_and(c >= 0, c < chunks))
            def _():
                frac_copy(u, c).start()

        @pl.when(k < chunks)
        def _():
            cur_copy(k).start()
            frac_copy(0, k).start()

        return 0

    land_copy(y).start()
    feed(jnp.int32(0))

    @pl.when(sends_relay)
    def _():
        relay_copy.start()

    lax.fori_loop(1, AHEAD, lambda k, z: feed(k), 0)
    for send, _, copy in halos:
        @pl.when(send)
        def _():
            copy.start()

    for u in range(steps):
        own_copy(u).wait()
    land_copy(other).wait_recv()

    target = lax.broadcasted_iota(jnp.int32, (hot_rows, 4 * rows * TILE), 0)

    def build(u, c):
        tile = lax.div(c, parts)

        @pl.when(lax.rem(c, parts) == 0)
        def _():
            picks = [target == land_buf[h, tile, pl.ds(steps - 1 - u, 1), :] for h in range(2)]
            picks = [jnp.where(pick, 1.0, 0.0).astype(jnp.bfloat16) for pick in picks]
            hot_buf[tile, u] = jnp.concatenate(picks, axis=1)

    def weights(u, c, piece=whole[0]):
        tables = []
        for h in range(2):
            f = frac_buf[(h, u, slice(None)) + place(c, 0, piece)]
            square = f * f
            rest = 1.0 - f
            w0 = rest * rest * (rest * (1.0 / 6.0))
            w1 = square * (0.5 * f - 1.0) + (2.0 / 3.0)
            w3 = square * (f * (1.0 / 6.0))
            tables.append((w0, w1, ((1.0 - w0) - w3) - w1, w3))
        return tables

    def splat(u, c, tables, values, piece=whole[0]):
        _, skip, wide = piece
        hot = hot_buf[lax.div(c, parts), u][: span * TILE]
        products = [
            (w * v).reshape(rows * TILE, wide) for table, v in zip(tables, values) for w in table
        ]
        high = [part.astype(jnp.bfloat16) for part in products]
        low = [(a - b.astype(jnp.float32)).astype(jnp.bfloat16) for a, b in zip(products, high)]
        out = jnp.dot(
            jnp.concatenate([hot, hot], axis=1),
            jnp.concatenate(high + low, axis=0),
            preferred_element_type=jnp.float32,
        )
        out = out.reshape(span, TILE, wide)
        lanes = pl.ds(skip, wide)
        tx_up[u, c, :, :, lanes] = out[BELOW + tall :]
        tx_dn[u, c, :, :, lanes] = out[:BELOW]

        @pl.when(has_upper)
        def _():
            up_copy(u, c, piece).start()

        @pl.when(has_lower)
        def _():
            dn_copy(u, c, piece).start()

        acc[c, :, :, lanes] = out[BELOW : BELOW + tall]

    def arrive(u, c, piece=whole[0]):
        @pl.when(has_lower)
        def _():
            up_copy(u, c, piece).wait_recv()

        @pl.when(has_upper)
        def _():
            dn_copy(u, c, piece).wait_recv()

    def combined(u, c, piece=whole[0]):
        lanes = pl.ds(piece[1], piece[2])
        own = acc[c, :, :, lanes]
        low = rx_lo[u, c, :, :, lanes]
        high = rx_hi[u, c, :, :, lanes]
        top = tall - BELOW
        sums = []
        for r in range(tall):
            total = own[r]
            if r < ABOVE:
                total = total + low[r]
            if r >= top:
                total = total + high[r - top]
            sums.append(total.astype(jnp.bfloat16).astype(jnp.float32))
        return sums

    def halves(c, u, piece=whole[0]):
        total = combined(u, c, piece)
        return jnp.stack(total[:rows]), jnp.stack(total[rows:])

    def start_splat(c):
        build(0, c)
        cur_copy(c).wait_recv()
        frac_copy(0, c).wait_recv()
        splat(0, c, weights(0, c), (cur[0, c], cur[1, c]))

    def finish(c, piece=whole[0]):
        lanes = pl.ds(piece[1], piece[2])
        arrive(steps - 1, c, piece)
        acc[c, :, :, lanes] = jnp.stack(combined(steps - 1, c, piece))
        back_copy(c, piece).start()
        adj_out[(slice(None),) + place(c, y * half, piece)] = acc[c, pl.ds(y * rows, rows), :, lanes]

    def advance(u, c):
        build(u, c)
        frac_copy(u, c).wait_recv()
        tables = weights(u, c)
        arrive(u - 1, c)
        splat(u, c, tables, halves(c, u - 1))

    grad_lane = lax.broadcasted_iota(jnp.int32, (cols, line), 1)

    def gradient(r):
        grad_out[0, r] = (img_pad[r + 2, TILE : TILE + cols] - img_pad[r, TILE : TILE + cols]) * 0.5
        grad_out[1, r] = (
            img_pad[r + 1, TILE + 1 : TILE + cols + 1] - img_pad[r + 1, TILE - 1 : TILE + cols - 1]
        ) * 0.5
        center = img_pad[r + 1, TILE : TILE + cols]
        after = jnp.where(grad_lane == line - 1, 0.0, pltpu.roll(center, line - 1, 1))
        before = jnp.where(grad_lane == 0, 0.0, pltpu.roll(center, 1, 1))
        grad_out[2, r] = (after - before) * 0.5

    def slot(k, z):
        feed(k + AHEAD)

        since = k - IMAGE_SLOT
        q = lax.div(since, IMAGE_GAP)
        turn = jnp.logical_and(since >= 0, lax.rem(since, IMAGE_GAP) == 0)

        @pl.when(jnp.logical_and(turn, q < tiles))
        def _():
            inner_copy(q).start()

            @pl.when(jnp.logical_and(gets_relay, q == 0))
            def _():
                relay_copy.wait_recv()

            @pl.when(gets_relay)
            def _():
                outer_copy(q).start()

        for u in range(steps - 1, 0, -1):
            c = k - offsets[u]

            @pl.when(jnp.logical_and(c >= 0, c < chunks))
            def _():
                advance(u, c)

        @pl.when(k < chunks)
        def _():
            start_splat(k)

        @pl.when(k >= offsets[steps])
        def _():
            finish(k - offsets[steps])

        return z

    feed(jnp.int32(AHEAD))
    start_splat(jnp.int32(0))
    lax.fori_loop(1, last_slot, slot, 0)

    final = jnp.int32(chunks - 1)
    if last_slot >= offsets[steps]:
        finish(jnp.int32(last_slot - offsets[steps]))
    build(steps - 1, final)
    frac_copy(steps - 1, final).wait_recv()
    arrive(steps - 2, final)
    for piece in split:
        splat(steps - 1, final, weights(steps - 1, final, piece), halves(final, steps - 2, piece), piece)

    image_copy.wait()
    for q in range(tiles):
        inner_copy(q).wait_recv()

        @pl.when(gets_outer)
        def _():
            outer_copy(q).wait_recv()

    @pl.when(jnp.logical_not(gets_outer))
    def _():
        img_pad[y * (rows + 1), TILE : TILE + cols] = jnp.zeros((cols, line), jnp.float32)

    for index, (_, receive, copy) in enumerate(halos):
        edge = 0 if index == 0 else cols + TILE

        @pl.when(receive)
        def _():
            copy.wait_recv()

        @pl.when(jnp.logical_not(receive))
        def _():
            img_pad[1 : rows + 1, edge : edge + TILE] = jnp.zeros((rows, TILE, line), jnp.float32)

    begin = last_slot + 1 - offsets[steps]

    def tail(c, z):
        finish(c)

        @pl.when(c - begin < rows)
        def _():
            gradient(c - begin)

        return z

    lax.fori_loop(begin, chunks - 1, tail, 0)
    for r in range(chunks - 1 - begin, rows):
        gradient(r)
    for piece in split:
        finish(final, piece)

    mine_half = pl.ds(pl.multiple_of(y * half, half), half)
    other_half = pl.ds(pl.multiple_of(other * half, half), half)
    land_copy(y).wait_send()
    remote(stage, cur.at[0], cur_send, cur_recv.at[0, 0], {"slab": partner}).wait_send()
    remote(
        frac_ref.at[:, :, :, other_half], frac_buf.at[0], frac_send, frac_recv.at[0, 0, 0], {"slab": partner}
    ).wait_send()

    @pl.when(has_upper)
    def _():
        remote(tx_up, rx_lo, up_send, up_recv.at[0, 0, 0], {"slab": s + 2}).wait_send()

    @pl.when(has_lower)
    def _():
        remote(tx_dn, rx_hi, dn_send, dn_recv.at[0, 0, 0], {"slab": s - 2}).wait_send()

    for q in range(tiles):
        inner_copy(q).wait_send()

        @pl.when(gets_relay)
        def _():
            outer_copy(q).wait_send()

    @pl.when(sends_relay)
    def _():
        relay_copy.wait_send()

    for send, _, copy in halos:
        @pl.when(send)
        def _():
            copy.wait_send()

    back_all = remote(
        adj_out.at[:, :, mine_half], adj_out.at[:, :, other_half], back_send, back_recv, {"slab": partner}
    )
    back_all.wait_recv()
    back_all.wait_send()


def forces(adj_ref, grad_ref, adj_out, force_out, adj_buf, force_buf, adj_sem, force_sem):
    copies = []
    for r in range(adj_ref.shape[0]):
        mine = adj_ref[r]
        for c in range(3):
            force_buf[c, r] = mine * grad_ref[c, r]
        copies.append(pltpu.make_async_copy(force_buf.at[:, r], force_out.at[:, r], force_sem.at[r]))
        copies[-1].start()
        adj_buf[r] = mine.astype(jnp.bfloat16)
        copies.append(pltpu.make_async_copy(adj_buf.at[r], adj_out.at[r], adj_sem.at[r]))
        copies[-1].start()
    for copy in copies:
        copy.wait()


def shards(slabs, pencils, final_adjoint, departure, fraction, image):
    steps, rows, cols = departure.shape
    line = image.shape[2]
    half = line // 2
    width = WIDTH if half % WIDTH == 0 else half
    tiles = cols // TILE
    chunks = tiles * (half // width)
    tall = 2 * rows
    hot_rows = -(-(BELOW + tall + ABOVE) * TILE // 16) * 16
    assert slabs % 2 == 0 and ABOVE <= tall and cols % (2 * TILE) == 0 and half % 128 == 0

    f32 = jnp.float32
    dma = pltpu.SemaphoreType.DMA
    vmem = pl.BlockSpec(memory_space=pltpu.VMEM)
    hbm = pl.BlockSpec(memory_space=pltpu.HBM)
    adjoint, gradient = pl.pallas_call(
        functools.partial(kernel, slabs, pencils),
        name="splat",
        out_shape=(
            jax.ShapeDtypeStruct((rows, cols, line), f32),
            jax.ShapeDtypeStruct((3, rows, cols, line), f32),
        ),
        in_specs=[hbm, hbm, hbm, hbm],
        out_specs=(vmem, vmem),
        scratch_shapes=[
            pltpu.VMEM((steps, rows, cols), jnp.int32),
            pltpu.VMEM((2, tiles, steps, 4 * rows * TILE), jnp.int32),
            pltpu.VMEM((rows, cols, line), jnp.bfloat16),
            pltpu.VMEM((chunks, rows, TILE, width), f32),
            pltpu.VMEM((2, chunks, rows, TILE, width), f32),
            pltpu.VMEM((2, steps, rows, cols, half), f32),
            pltpu.VMEM((tiles, steps, hot_rows, 8 * rows * TILE), jnp.bfloat16),
            pltpu.VMEM((chunks, tall, TILE, width), f32),
            pltpu.VMEM((steps, chunks, ABOVE, TILE, width), f32),
            pltpu.VMEM((steps, chunks, BELOW, TILE, width), f32),
            pltpu.VMEM((steps, chunks, ABOVE, TILE, width), f32),
            pltpu.VMEM((steps, chunks, BELOW, TILE, width), f32),
            pltpu.VMEM((rows + 2, cols + 2 * TILE, line), f32),
            pltpu.VMEM((1, cols, line), f32),
            dma(()),
            dma((2,)),
            dma(()),
            dma(()),
            dma((chunks, 2)),
            dma((steps,)),
            dma(()),
            dma((steps, chunks, 2)),
            dma(()),
            dma((steps, chunks, 2)),
            dma(()),
            dma((steps, chunks, 2)),
            dma(()),
            dma(()),
            dma(()),
            dma((2, 3)),
            dma((2, tiles)),
            dma((2, tiles)),
        ],
        compiler_params=pltpu.CompilerParams(
            collective_id=0, has_side_effects=True, vmem_limit_bytes=40 * 1024 * 1024
        ),
    )(*(pltpu.with_memory_space_constraint(a, pltpu.HBM) for a in (departure, final_adjoint, fraction, image)))
    return pl.pallas_call(
        forces,
        name="forces",
        out_shape=(
            jax.ShapeDtypeStruct((rows, cols, line), jnp.bfloat16),
            jax.ShapeDtypeStruct((3, rows, cols, line), f32),
        ),
        in_specs=[vmem, vmem],
        out_specs=(hbm, hbm),
        scratch_shapes=[
            pltpu.VMEM((rows, cols, line), jnp.bfloat16),
            pltpu.VMEM((3, rows, cols, line), f32),
            dma((rows,)),
            dma((rows,)),
        ],
        compiler_params=pltpu.CompilerParams(vmem_limit_bytes=16 * 1024 * 1024),
    )(adjoint, gradient)


def solution(mesh):
    in_specs = (
        P("slab", "pencil", None),
        P(None, "slab", "pencil"),
        P(None, "slab", "pencil", None),
        P("slab", "pencil", None),
    )
    out_specs = (P("slab", "pencil", None), P(None, "slab", "pencil", None))
    body = functools.partial(shards, mesh.shape["slab"], mesh.shape["pencil"])
    return jax.shard_map(body, mesh=mesh, in_specs=in_specs, out_specs=out_specs, check_vma=False)
```

```python
import functools

import jax
import jax.numpy as jnp
from jax import lax
from jax.experimental import pallas as pl
from jax.experimental.pallas import tpu as pltpu
from jax.sharding import PartitionSpec as P

BELOW = 5
ABOVE = 6
TILE = 8
WIDTH = 256
OFFSETS = (0, 3, 8, 14, 20)
AHEAD = 12
IMAGE_SLOT = 14
IMAGE_GAP = 1
SPLIT = True
GRADIENT_SLOT = 2
MESH = pl.DeviceIdType.MESH


def kernel(
    slabs,
    pencils,
    dep_ref,
    adj_ref,
    frac_ref,
    img_ref,
    adj_out,
    grad_out,
    dep_buf,
    land_buf,
    adj_buf,
    stage,
    cur,
    frac_buf,
    hot_buf,
    acc,
    tx_up,
    tx_dn,
    rx_lo,
    rx_hi,
    img_pad,
    relay_buf,
    dep_sem,
    land_sem,
    adj_sem,
    cur_send,
    cur_recv,
    own_sem,
    frac_send,
    frac_recv,
    up_send,
    up_recv,
    dn_send,
    dn_recv,
    back_send,
    back_recv,
    img_sem,
    halo_sem,
    inner_sem,
    outer_sem,
):
    s = lax.axis_index("slab")
    p = lax.axis_index("pencil")
    y = lax.rem(s, 2)
    other = 1 - y
    partner = s + 1 - 2 * y
    pair = lax.div(s, 2)
    has_lower = s >= 2
    has_upper = s + 2 < slabs

    rows, cols, line = adj_out.shape
    half = line // 2
    width = stage.shape[-1]
    hot_rows = hot_buf.shape[2]
    parts = half // width
    tiles = cols // TILE
    chunks = tiles * parts
    steps = frac_ref.shape[0]
    tall = 2 * rows
    span = BELOW + tall + ABOVE
    offsets = OFFSETS if steps == 4 and chunks == 8 else tuple(u * chunks for u in range(steps + 1))
    last_slot = chunks - 1 + offsets[steps - 1]
    whole = ((0, 0, width),)
    split = ((0, 0, width // 2), (1, width // 2, width // 2)) if SPLIT and width % 256 == 0 else whole

    def remote(src, dst, send_sem, recv_sem, where):
        return pltpu.make_async_remote_copy(
            src_ref=src,
            dst_ref=dst,
            send_sem=send_sem,
            recv_sem=recv_sem,
            device_id=where,
            device_id_type=MESH,
        )

    def place(c, start, piece=whole[0]):
        _, skip, wide = piece
        first = pl.multiple_of(lax.div(c, parts) * TILE, TILE)
        lanes = pl.multiple_of(start + lax.rem(c, parts) * width + skip, wide)
        return pl.ds(first, TILE), pl.ds(lanes, wide)

    def cut(ref, at, piece):
        return ref.at[at + (slice(None), slice(None), pl.ds(piece[1], piece[2]))]

    def own_copy(u):
        return pltpu.make_async_copy(
            frac_ref.at[steps - 1 - u, :, :, pl.ds(pl.multiple_of(y * half, half), half)],
            frac_buf.at[y, u],
            own_sem.at[u],
        )

    def frac_copy(u, c, piece=whole[0]):
        return remote(
            frac_ref.at[(steps - 1 - u, slice(None)) + place(c, other * half, piece)],
            frac_buf.at[(y, u, slice(None)) + place(c, 0, piece)],
            frac_send,
            frac_recv.at[u, c, piece[0]],
            {"slab": partner},
        )

    def cur_copy(c, piece=whole[0]):
        return remote(
            cut(stage, (c,), piece), cut(cur, (y, c), piece), cur_send, cur_recv.at[c, piece[0]], {"slab": partner}
        )

    def land_copy(h):
        return remote(land_buf.at[h], land_buf.at[h], land_sem.at[0], land_sem.at[1], {"slab": partner})

    def up_copy(u, c, piece=whole[0]):
        return remote(
            cut(tx_up, (u, c), piece), cut(rx_lo, (u, c), piece), up_send, up_recv.at[u, c, piece[0]], {"slab": s + 2}
        )

    def dn_copy(u, c, piece=whole[0]):
        return remote(
            cut(tx_dn, (u, c), piece), cut(rx_hi, (u, c), piece), dn_send, dn_recv.at[u, c, piece[0]], {"slab": s - 2}
        )

    def back_copy(c, piece=whole[0]):
        return remote(
            acc.at[c, pl.ds(other * rows, rows), :, pl.ds(piece[1], piece[2])],
            adj_out.at[(slice(None),) + place(c, y * half, piece)],
            back_send,
            back_recv,
            {"slab": partner},
        )

    center_cols = pl.ds(TILE, cols)
    image_copy = pltpu.make_async_copy(
        img_ref, img_pad.at[pl.ds(1, rows), center_cols], img_sem
    )
    relay_to = s + 4 * y - 2
    relay_from = s + 2 - 4 * y
    outer = s + 2 * y - 1
    sends_relay = jnp.logical_and(relay_to >= 0, relay_to < slabs)
    gets_relay = jnp.logical_and(relay_from >= 0, relay_from < slabs)
    gets_outer = jnp.logical_and(outer >= 0, outer < slabs)

    def halo(src, dst, index, where):
        return remote(src, dst, halo_sem.at[0, index], halo_sem.at[1, index], where)

    relay_copy = halo(img_ref.at[pl.ds(y * (rows - 1), 1)], relay_buf, 0, {"slab": relay_to})

    def edge_copy(row, src, src_row, sems, q):
        first = pl.multiple_of(q * TILE, TILE)
        return remote(
            src.at[pl.ds(src_row, 1), pl.ds(first, TILE)],
            img_pad.at[pl.ds(row, 1), pl.ds(pl.multiple_of(first + TILE, TILE), TILE)],
            sems.at[0, q],
            sems.at[1, q],
            {"slab": partner},
        )

    def outer_copy(q):
        return edge_copy(other * (rows + 1), relay_buf, 0, outer_sem, q)

    def inner_copy(q):
        return edge_copy(y * (rows + 1), img_ref, other * (rows - 1), inner_sem, q)

    halos = (
        (p + 1 < pencils, p >= 1, halo(
            img_ref.at[:, pl.ds(cols - TILE, TILE)], img_pad.at[pl.ds(1, rows), pl.ds(0, TILE)],
            1, {"pencil": p + 1})),
        (p >= 1, p + 1 < pencils, halo(
            img_ref.at[:, pl.ds(0, TILE)], img_pad.at[pl.ds(1, rows), pl.ds(cols + TILE, TILE)],
            2, {"pencil": p - 1})),
    )

    barrier = pltpu.get_barrier_semaphore()
    for there, where in (
        (slabs > 1, {"slab": partner}),
        (has_lower, {"slab": s - 2}),
        (has_upper, {"slab": s + 2}),
        (p >= 1, {"pencil": p - 1}),
        (p + 1 < pencils, {"pencil": p + 1}),
    ):
        @pl.when(there)
        def _():
            pl.semaphore_signal(barrier, inc=1, device_id=where, device_id_type=MESH)

    adj_copy = pltpu.make_async_copy(adj_ref, adj_buf, adj_sem)
    dep_copy = pltpu.make_async_copy(dep_ref, dep_buf, dep_sem)
    dep_copy.start()
    adj_copy.start()
    for u in range(steps):
        own_copy(u).start()
    image_copy.start()

    lane = lax.broadcasted_iota(jnp.int32, (steps, 4 * rows * TILE), 1)
    lane_row = lax.rem(lax.div(lane, TILE), rows)
    fixed = lane_row + lax.div(lane, rows * TILE) - 1 + BELOW
    fixed = fixed * TILE + lax.rem(lane, TILE)
    pick_lane = lax.broadcasted_iota(jnp.int32, (cols, 4 * rows * TILE), 1)
    pick_col = lax.broadcasted_iota(jnp.int32, (cols, 4 * rows * TILE), 0)
    keep_lane = lax.broadcasted_iota(jnp.int32, (steps * rows, 4 * rows * TILE), 1)
    keep_row = lax.broadcasted_iota(jnp.int32, (steps * rows, 4 * rows * TILE), 0)
    keep = lax.rem(keep_row, rows) == lax.rem(lax.div(keep_lane, TILE), rows)
    group_step = lax.broadcasted_iota(jnp.int32, (steps, steps * rows), 0)
    group_row = lax.broadcasted_iota(jnp.int32, (steps, steps * rows), 1)
    group = jnp.where(group_step == lax.div(group_row, rows), 1.0, 0.0).astype(jnp.bfloat16)
    row_of = lax.broadcasted_iota(jnp.int32, (rows, cols), 0)

    def landing(h):
        first_row = pair * tall + h * rows
        moved = jnp.concatenate([dep_buf[k] - row_of - first_row for k in range(steps)], axis=0)
        moved = moved.astype(jnp.float32).astype(jnp.bfloat16)
        for tile in range(tiles):
            pick = pick_col == tile * TILE + lax.rem(pick_lane, TILE)
            pick = jnp.where(pick, 1.0, 0.0).astype(jnp.bfloat16)
            spread = jnp.dot(moved, pick, preferred_element_type=jnp.float32)
            spread = jnp.where(keep, spread, 0.0).astype(jnp.bfloat16)
            by_step = jnp.dot(group, spread, preferred_element_type=jnp.float32)
            land_buf[h, tile] = fixed + h * rows * TILE + by_step.astype(jnp.int32) * TILE

    adj_copy.wait()
    for q in range(cols // (2 * TILE)):
        for h in range(2):
            for k in range(parts):
                lanes = pl.ds(pl.multiple_of((y if h == 0 else other) * half + width * k, width), width)
                wide = adj_buf[:, 2 * TILE * q : 2 * TILE * (q + 1), lanes].astype(jnp.float32)
                if h == 0:
                    cur[y, 2 * q * parts + k] = wide[:, :TILE]
                    cur[y, (2 * q + 1) * parts + k] = wide[:, TILE:]
                else:
                    stage[2 * q * parts + k] = wide[:, :TILE]
                    stage[(2 * q + 1) * parts + k] = wide[:, TILE:]
    dep_copy.wait()
    landing(y)

    @pl.when(jnp.logical_not(has_lower))
    def _():
        rx_lo[...] = jnp.zeros_like(rx_lo)

    @pl.when(jnp.logical_not(has_upper))
    def _():
        rx_hi[...] = jnp.zeros_like(rx_hi)


    peers = sum(
        jnp.where(there, 1, 0)
        for there in (slabs > 1, has_lower, has_upper, p >= 1, p + 1 < pencils)
    )
    pl.semaphore_wait(barrier, peers)

    def feed(k):
        for u in range(steps - 1, 0, -1):
            c = k - offsets[u]

            @pl.when(jnp.logical_and(c >= 0, c < chunks))
            def _():
                frac_copy(u, c).start()

        @pl.when(k < chunks)
        def _():
            cur_copy(k).start()
            frac_copy(0, k).start()

        return 0

    land_copy(y).start()
    feed(jnp.int32(0))

    @pl.when(sends_relay)
    def _():
        relay_copy.start()

    lax.fori_loop(1, AHEAD, lambda k, z: feed(k), 0)
    for send, _, copy in halos:
        @pl.when(send)
        def _():
            copy.start()

    for u in range(steps):
        own_copy(u).wait()
    land_copy(other).wait_recv()

    target = lax.broadcasted_iota(jnp.int32, (hot_rows, 4 * rows * TILE), 0)

    def build(u, c):
        tile = lax.div(c, parts)

        @pl.when(lax.rem(c, parts) == 0)
        def _():
            picks = [target == land_buf[h, tile, pl.ds(steps - 1 - u, 1), :] for h in range(2)]
            picks = [jnp.where(pick, 1.0, 0.0).astype(jnp.bfloat16) for pick in picks]
            hot_buf[tile, u] = jnp.concatenate(picks, axis=1)

    def weights(u, c, piece=whole[0]):
        tables = []
        for h in range(2):
            f = frac_buf[(h, u, slice(None)) + place(c, 0, piece)]
            square = f * f
            rest = 1.0 - f
            w0 = rest * rest * (rest * (1.0 / 6.0))
            w1 = square * (0.5 * f - 1.0) + (2.0 / 3.0)
            w3 = square * (f * (1.0 / 6.0))
            tables.append((w0, w1, ((1.0 - w0) - w3) - w1, w3))
        return tables

    def splat(u, c, tables, values, piece=whole[0]):
        _, skip, wide = piece
        hot = hot_buf[lax.div(c, parts), u]
        products = [
            (w * v).reshape(rows * TILE, wide) for table, v in zip(tables, values) for w in table
        ]
        high = [part.astype(jnp.bfloat16) for part in products]
        low = [(a - b.astype(jnp.float32)).astype(jnp.bfloat16) for a, b in zip(products, high)]
        out = jnp.dot(
            jnp.concatenate([hot, hot], axis=1),
            jnp.concatenate(high + low, axis=0),
            preferred_element_type=jnp.float32,
        )
        out = out[: span * TILE].reshape(span, TILE, wide)
        lanes = pl.ds(skip, wide)
        tx_up[u, c, :, :, lanes] = out[BELOW + tall :]
        tx_dn[u, c, :, :, lanes] = out[:BELOW]

        @pl.when(has_upper)
        def _():
            up_copy(u, c, piece).start()

        @pl.when(has_lower)
        def _():
            dn_copy(u, c, piece).start()

        acc[c, :, :, lanes] = out[BELOW : BELOW + tall]

    def arrive(u, c, piece=whole[0]):
        @pl.when(has_lower)
        def _():
            up_copy(u, c, piece).wait_recv()

        @pl.when(has_upper)
        def _():
            dn_copy(u, c, piece).wait_recv()

    def combined(u, c, piece=whole[0]):
        lanes = pl.ds(piece[1], piece[2])
        own = acc[c, :, :, lanes]
        low = rx_lo[u, c, :, :, lanes]
        high = rx_hi[u, c, :, :, lanes]
        top = tall - BELOW
        sums = []
        for r in range(tall):
            total = own[r]
            if r < ABOVE:
                total = total + low[r]
            if r >= top:
                total = total + high[r - top]
            sums.append(total.astype(jnp.bfloat16).astype(jnp.float32))
        return sums

    def halves(c, u, piece=whole[0]):
        total = combined(u, c, piece)
        return jnp.stack(total[:rows]), jnp.stack(total[rows:])

    def start_splat(c):
        build(0, c)
        cur_copy(c).wait_recv()
        frac_copy(0, c).wait_recv()
        splat(0, c, weights(0, c), (cur[0, c], cur[1, c]))

    def finish(c, piece=whole[0]):
        lanes = pl.ds(piece[1], piece[2])
        arrive(steps - 1, c, piece)
        acc[c, :, :, lanes] = jnp.stack(combined(steps - 1, c, piece))
        back_copy(c, piece).start()
        adj_out[(slice(None),) + place(c, y * half, piece)] = acc[c, pl.ds(y * rows, rows), :, lanes]

    def advance(u, c):
        build(u, c)
        frac_copy(u, c).wait_recv()
        tables = weights(u, c)
        arrive(u - 1, c)
        splat(u, c, tables, halves(c, u - 1))

    grad_lane = lax.broadcasted_iota(jnp.int32, (cols, line), 1)

    def across(r):
        grad_out[0, r] = (img_pad[r + 2, TILE : TILE + cols] - img_pad[r, TILE : TILE + cols]) * 0.5

    def gradient(r):
        @pl.when(jnp.logical_and(r >= 1, r < rows - 1))
        def _():
            across(r)

        grad_out[1, r] = (
            img_pad[r + 1, TILE + 1 : TILE + cols + 1] - img_pad[r + 1, TILE - 1 : TILE + cols - 1]
        ) * 0.5
        center = img_pad[r + 1, TILE : TILE + cols]
        after = jnp.where(grad_lane == line - 1, 0.0, pltpu.roll(center, line - 1, 1))
        before = jnp.where(grad_lane == 0, 0.0, pltpu.roll(center, 1, 1))
        grad_out[2, r] = (after - before) * 0.5

    def borders():
        image_copy.wait()
        for index, (_, receive, copy) in enumerate(halos):
            edge = 0 if index == 0 else cols + TILE

            @pl.when(receive)
            def _():
                copy.wait_recv()

            @pl.when(jnp.logical_not(receive))
            def _():
                img_pad[1 : rows + 1, edge : edge + TILE] = jnp.zeros((rows, TILE, line), jnp.float32)

    def slot(k, z):
        feed(k + AHEAD)

        since = k - IMAGE_SLOT
        q = lax.div(since, IMAGE_GAP)
        turn = jnp.logical_and(since >= 0, lax.rem(since, IMAGE_GAP) == 0)

        @pl.when(jnp.logical_and(turn, q < tiles))
        def _():
            inner_copy(q).start()

            @pl.when(jnp.logical_and(gets_relay, q == 0))
            def _():
                relay_copy.wait_recv()

            @pl.when(gets_relay)
            def _():
                outer_copy(q).start()

        for u in range(steps - 1, 0, -1):
            c = k - offsets[u]

            @pl.when(jnp.logical_and(c >= 0, c < chunks))
            def _():
                advance(u, c)

        @pl.when(k < chunks)
        def _():
            start_splat(k)

        @pl.when(k >= offsets[steps])
        def _():
            finish(k - offsets[steps])

        row = k - GRADIENT_SLOT

        @pl.when(row == 0)
        def _():
            borders()

        @pl.when(jnp.logical_and(row >= 0, row < rows))
        def _():
            gradient(row)

        return z

    feed(jnp.int32(AHEAD))
    start_splat(jnp.int32(0))
    lax.fori_loop(1, last_slot, slot, 0)

    final = jnp.int32(chunks - 1)
    if last_slot >= offsets[steps]:
        finish(jnp.int32(last_slot - offsets[steps]))
    build(steps - 1, final)
    frac_copy(steps - 1, final).wait_recv()
    arrive(steps - 2, final)
    for piece in split:
        splat(steps - 1, final, weights(steps - 1, final, piece), halves(final, steps - 2, piece), piece)

    begin = last_slot + 1 - offsets[steps]

    def tail(c, z):
        finish(c)

        return z

    lax.fori_loop(begin, chunks - 1, tail, 0)
    for piece in split:
        finish(final, piece)

    for q in range(tiles):
        inner_copy(q).wait_recv()

        @pl.when(gets_outer)
        def _():
            outer_copy(q).wait_recv()

    @pl.when(jnp.logical_not(gets_outer))
    def _():
        img_pad[y * (rows + 1), TILE : TILE + cols] = jnp.zeros((cols, line), jnp.float32)

    across(0)
    across(rows - 1)

    mine_half = pl.ds(pl.multiple_of(y * half, half), half)
    other_half = pl.ds(pl.multiple_of(other * half, half), half)
    land_copy(y).wait_send()
    remote(stage, cur.at[0], cur_send, cur_recv.at[0, 0], {"slab": partner}).wait_send()
    remote(
        frac_ref.at[:, :, :, other_half], frac_buf.at[0], frac_send, frac_recv.at[0, 0, 0], {"slab": partner}
    ).wait_send()

    @pl.when(has_upper)
    def _():
        remote(tx_up, rx_lo, up_send, up_recv.at[0, 0, 0], {"slab": s + 2}).wait_send()

    @pl.when(has_lower)
    def _():
        remote(tx_dn, rx_hi, dn_send, dn_recv.at[0, 0, 0], {"slab": s - 2}).wait_send()

    for q in range(tiles):
        inner_copy(q).wait_send()

        @pl.when(gets_relay)
        def _():
            outer_copy(q).wait_send()

    @pl.when(sends_relay)
    def _():
        relay_copy.wait_send()

    for send, _, copy in halos:
        @pl.when(send)
        def _():
            copy.wait_send()

    back_all = remote(
        adj_out.at[:, :, mine_half], adj_out.at[:, :, other_half], back_send, back_recv, {"slab": partner}
    )
    back_all.wait_recv()
    back_all.wait_send()


def forces(adj_ref, grad_ref, adj_out, force_out, adj_buf, force_buf, adj_sem, force_sem):
    copies = []
    for r in range(adj_ref.shape[0]):
        mine = adj_ref[r]
        for c in range(3):
            force_buf[c, r] = mine * grad_ref[c, r]
        copies.append(pltpu.make_async_copy(force_buf.at[:, r], force_out.at[:, r], force_sem.at[r]))
        copies[-1].start()
        adj_buf[r] = mine.astype(jnp.bfloat16)
        copies.append(pltpu.make_async_copy(adj_buf.at[r], adj_out.at[r], adj_sem.at[r]))
        copies[-1].start()
    for copy in copies:
        copy.wait()


def shards(slabs, pencils, final_adjoint, departure, fraction, image):
    steps, rows, cols = departure.shape
    line = image.shape[2]
    half = line // 2
    width = WIDTH if half % WIDTH == 0 else half
    tiles = cols // TILE
    chunks = tiles * (half // width)
    tall = 2 * rows
    assert GRADIENT_SLOT + rows <= 3 * chunks
    hot_rows = -(-(BELOW + tall + ABOVE) * TILE // 16) * 16
    assert slabs % 2 == 0 and ABOVE <= tall and cols % (2 * TILE) == 0 and half % 128 == 0

    f32 = jnp.float32
    dma = pltpu.SemaphoreType.DMA
    vmem = pl.BlockSpec(memory_space=pltpu.VMEM)
    hbm = pl.BlockSpec(memory_space=pltpu.HBM)
    adjoint, gradient = pl.pallas_call(
        functools.partial(kernel, slabs, pencils),
        name="splat",
        out_shape=(
            jax.ShapeDtypeStruct((rows, cols, line), f32),
            jax.ShapeDtypeStruct((3, rows, cols, line), f32),
        ),
        in_specs=[hbm, hbm, hbm, hbm],
        out_specs=(vmem, vmem),
        scratch_shapes=[
            pltpu.VMEM((steps, rows, cols), jnp.int32),
            pltpu.VMEM((2, tiles, steps, 4 * rows * TILE), jnp.int32),
            pltpu.VMEM((rows, cols, line), jnp.bfloat16),
            pltpu.VMEM((chunks, rows, TILE, width), f32),
            pltpu.VMEM((2, chunks, rows, TILE, width), f32),
            pltpu.VMEM((2, steps, rows, cols, half), f32),
            pltpu.VMEM((tiles, steps, hot_rows, 8 * rows * TILE), jnp.bfloat16),
            pltpu.VMEM((chunks, tall, TILE, width), f32),
            pltpu.VMEM((steps, chunks, ABOVE, TILE, width), f32),
            pltpu.VMEM((steps, chunks, BELOW, TILE, width), f32),
            pltpu.VMEM((steps, chunks, ABOVE, TILE, width), f32),
            pltpu.VMEM((steps, chunks, BELOW, TILE, width), f32),
            pltpu.VMEM((rows + 2, cols + 2 * TILE, line), f32),
            pltpu.VMEM((1, cols, line), f32),
            dma(()),
            dma((2,)),
            dma(()),
            dma(()),
            dma((chunks, 2)),
            dma((steps,)),
            dma(()),
            dma((steps, chunks, 2)),
            dma(()),
            dma((steps, chunks, 2)),
            dma(()),
            dma((steps, chunks, 2)),
            dma(()),
            dma(()),
            dma(()),
            dma((2, 3)),
            dma((2, tiles)),
            dma((2, tiles)),
        ],
        compiler_params=pltpu.CompilerParams(
            collective_id=0, has_side_effects=True, vmem_limit_bytes=40 * 1024 * 1024
        ),
    )(*(pltpu.with_memory_space_constraint(a, pltpu.HBM) for a in (departure, final_adjoint, fraction, image)))
    return pl.pallas_call(
        forces,
        name="forces",
        out_shape=(
            jax.ShapeDtypeStruct((rows, cols, line), jnp.bfloat16),
            jax.ShapeDtypeStruct((3, rows, cols, line), f32),
        ),
        in_specs=[vmem, vmem],
        out_specs=(hbm, hbm),
        scratch_shapes=[
            pltpu.VMEM((rows, cols, line), jnp.bfloat16),
            pltpu.VMEM((3, rows, cols, line), f32),
            dma((rows,)),
            dma((rows,)),
        ],
        compiler_params=pltpu.CompilerParams(vmem_limit_bytes=16 * 1024 * 1024),
    )(adjoint, gradient)


def solution(mesh):
    in_specs = (
        P("slab", "pencil", None),
        P(None, "slab", "pencil"),
        P(None, "slab", "pencil", None),
        P("slab", "pencil", None),
    )
    out_specs = (P("slab", "pencil", None), P(None, "slab", "pencil", None))
    body = functools.partial(shards, mesh.shape["slab"], mesh.shape["pencil"])
    return jax.shard_map(body, mesh=mesh, in_specs=in_specs, out_specs=out_specs, check_vma=False)
```

```python
import functools

import jax
import jax.numpy as jnp
from jax import lax
from jax.experimental import pallas as pl
from jax.experimental.pallas import tpu as pltpu
from jax.sharding import PartitionSpec as P

BELOW = 5
ABOVE = 6
TILE = 8
WIDTH = 256
OFFSETS = (0, 3, 8, 13, 19)
AHEAD = 12
IMAGE_SLOT = 14
IMAGE_GAP = 1
SPLIT = True
GRADIENT_SLOT = 2
MESH = pl.DeviceIdType.MESH


def kernel(
    slabs,
    pencils,
    dep_ref,
    adj_ref,
    frac_ref,
    img_ref,
    adj_out,
    grad_out,
    dep_buf,
    land_buf,
    adj_buf,
    stage,
    cur,
    frac_buf,
    hot_buf,
    acc,
    tx_up,
    tx_dn,
    rx_lo,
    rx_hi,
    img_pad,
    relay_buf,
    dep_sem,
    land_sem,
    adj_sem,
    cur_send,
    cur_recv,
    own_sem,
    frac_send,
    frac_recv,
    up_send,
    up_recv,
    dn_send,
    dn_recv,
    back_send,
    back_recv,
    img_sem,
    halo_sem,
    inner_sem,
    outer_sem,
):
    s = lax.axis_index("slab")
    p = lax.axis_index("pencil")
    y = lax.rem(s, 2)
    other = 1 - y
    partner = s + 1 - 2 * y
    pair = lax.div(s, 2)
    has_lower = s >= 2
    has_upper = s + 2 < slabs

    rows, cols, line = adj_out.shape
    half = line // 2
    width = stage.shape[-1]
    hot_rows = hot_buf.shape[2]
    parts = half // width
    tiles = cols // TILE
    chunks = tiles * parts
    steps = frac_ref.shape[0]
    tall = 2 * rows
    span = BELOW + tall + ABOVE
    offsets = OFFSETS if steps == 4 and chunks == 8 else tuple(u * chunks for u in range(steps + 1))
    last_slot = chunks - 1 + offsets[steps - 1]
    whole = ((0, 0, width),)
    split = ((0, 0, width // 2), (1, width // 2, width // 2)) if SPLIT and width % 256 == 0 else whole

    def remote(src, dst, send_sem, recv_sem, where):
        return pltpu.make_async_remote_copy(
            src_ref=src,
            dst_ref=dst,
            send_sem=send_sem,
            recv_sem=recv_sem,
            device_id=where,
            device_id_type=MESH,
        )

    def place(c, start, piece=whole[0]):
        _, skip, wide = piece
        first = pl.multiple_of(lax.div(c, parts) * TILE, TILE)
        lanes = pl.multiple_of(start + lax.rem(c, parts) * width + skip, wide)
        return pl.ds(first, TILE), pl.ds(lanes, wide)

    def cut(ref, at, piece):
        return ref.at[at + (slice(None), slice(None), pl.ds(piece[1], piece[2]))]

    def own_copy(u):
        return pltpu.make_async_copy(
            frac_ref.at[steps - 1 - u, :, :, pl.ds(pl.multiple_of(y * half, half), half)],
            frac_buf.at[y, u],
            own_sem.at[u],
        )

    def frac_copy(u, c, piece=whole[0]):
        return remote(
            frac_ref.at[(steps - 1 - u, slice(None)) + place(c, other * half, piece)],
            frac_buf.at[(y, u, slice(None)) + place(c, 0, piece)],
            frac_send,
            frac_recv.at[u, c, piece[0]],
            {"slab": partner},
        )

    def cur_copy(c, piece=whole[0]):
        return remote(
            cut(stage, (c,), piece), cut(cur, (y, c), piece), cur_send, cur_recv.at[c, piece[0]], {"slab": partner}
        )

    def land_copy(h):
        return remote(land_buf.at[h], land_buf.at[h], land_sem.at[0], land_sem.at[1], {"slab": partner})

    def up_copy(u, c, piece=whole[0]):
        return remote(
            cut(tx_up, (u, c), piece), cut(rx_lo, (u, c), piece), up_send, up_recv.at[u, c, piece[0]], {"slab": s + 2}
        )

    def dn_copy(u, c, piece=whole[0]):
        return remote(
            cut(tx_dn, (u, c), piece), cut(rx_hi, (u, c), piece), dn_send, dn_recv.at[u, c, piece[0]], {"slab": s - 2}
        )

    def back_copy(c, piece=whole[0]):
        return remote(
            acc.at[c, pl.ds(other * rows, rows), :, pl.ds(piece[1], piece[2])],
            adj_out.at[(slice(None),) + place(c, y * half, piece)],
            back_send,
            back_recv,
            {"slab": partner},
        )

    center_cols = pl.ds(TILE, cols)
    image_copy = pltpu.make_async_copy(
        img_ref, img_pad.at[pl.ds(1, rows), center_cols], img_sem
    )
    relay_to = s + 4 * y - 2
    relay_from = s + 2 - 4 * y
    outer = s + 2 * y - 1
    sends_relay = jnp.logical_and(relay_to >= 0, relay_to < slabs)
    gets_relay = jnp.logical_and(relay_from >= 0, relay_from < slabs)
    gets_outer = jnp.logical_and(outer >= 0, outer < slabs)

    def halo(src, dst, index, where):
        return remote(src, dst, halo_sem.at[0, index], halo_sem.at[1, index], where)

    relay_copy = halo(img_ref.at[pl.ds(y * (rows - 1), 1)], relay_buf, 0, {"slab": relay_to})

    def edge_copy(row, src, src_row, sems, q):
        first = pl.multiple_of(q * TILE, TILE)
        return remote(
            src.at[pl.ds(src_row, 1), pl.ds(first, TILE)],
            img_pad.at[pl.ds(row, 1), pl.ds(pl.multiple_of(first + TILE, TILE), TILE)],
            sems.at[0, q],
            sems.at[1, q],
            {"slab": partner},
        )

    def outer_copy(q):
        return edge_copy(other * (rows + 1), relay_buf, 0, outer_sem, q)

    def inner_copy(q):
        return edge_copy(y * (rows + 1), img_ref, other * (rows - 1), inner_sem, q)

    halos = (
        (p + 1 < pencils, p >= 1, halo(
            img_ref.at[:, pl.ds(cols - TILE, TILE)], img_pad.at[pl.ds(1, rows), pl.ds(0, TILE)],
            1, {"pencil": p + 1})),
        (p >= 1, p + 1 < pencils, halo(
            img_ref.at[:, pl.ds(0, TILE)], img_pad.at[pl.ds(1, rows), pl.ds(cols + TILE, TILE)],
            2, {"pencil": p - 1})),
    )

    barrier = pltpu.get_barrier_semaphore()
    for there, where in (
        (slabs > 1, {"slab": partner}),
        (has_lower, {"slab": s - 2}),
        (has_upper, {"slab": s + 2}),
        (p >= 1, {"pencil": p - 1}),
        (p + 1 < pencils, {"pencil": p + 1}),
    ):
        @pl.when(there)
        def _():
            pl.semaphore_signal(barrier, inc=1, device_id=where, device_id_type=MESH)

    adj_copy = pltpu.make_async_copy(adj_ref, adj_buf, adj_sem)
    dep_copy = pltpu.make_async_copy(dep_ref, dep_buf, dep_sem)
    dep_copy.start()
    adj_copy.start()
    for u in range(steps):
        own_copy(u).start()
    image_copy.start()

    lane = lax.broadcasted_iota(jnp.int32, (steps, 4 * rows * TILE), 1)
    lane_row = lax.rem(lax.div(lane, TILE), rows)
    fixed = lane_row + lax.div(lane, rows * TILE) - 1 + BELOW
    fixed = fixed * TILE + lax.rem(lane, TILE)
    pick_lane = lax.broadcasted_iota(jnp.int32, (cols, 4 * rows * TILE), 1)
    pick_col = lax.broadcasted_iota(jnp.int32, (cols, 4 * rows * TILE), 0)
    keep_lane = lax.broadcasted_iota(jnp.int32, (steps * rows, 4 * rows * TILE), 1)
    keep_row = lax.broadcasted_iota(jnp.int32, (steps * rows, 4 * rows * TILE), 0)
    keep = lax.rem(keep_row, rows) == lax.rem(lax.div(keep_lane, TILE), rows)
    group_step = lax.broadcasted_iota(jnp.int32, (steps, steps * rows), 0)
    group_row = lax.broadcasted_iota(jnp.int32, (steps, steps * rows), 1)
    group = jnp.where(group_step == lax.div(group_row, rows), 1.0, 0.0).astype(jnp.bfloat16)
    row_of = lax.broadcasted_iota(jnp.int32, (rows, cols), 0)

    def landing(h):
        first_row = pair * tall + h * rows
        moved = jnp.concatenate([dep_buf[k] - row_of - first_row for k in range(steps)], axis=0)
        moved = moved.astype(jnp.float32).astype(jnp.bfloat16)
        for tile in range(tiles):
            pick = pick_col == tile * TILE + lax.rem(pick_lane, TILE)
            pick = jnp.where(pick, 1.0, 0.0).astype(jnp.bfloat16)
            spread = jnp.dot(moved, pick, preferred_element_type=jnp.float32)
            spread = jnp.where(keep, spread, 0.0).astype(jnp.bfloat16)
            by_step = jnp.dot(group, spread, preferred_element_type=jnp.float32)
            land_buf[h, tile] = fixed + h * rows * TILE + by_step.astype(jnp.int32) * TILE

    adj_copy.wait()
    for q in range(cols // (2 * TILE)):
        for h in range(2):
            for k in range(parts):
                lanes = pl.ds(pl.multiple_of((y if h == 0 else other) * half + width * k, width), width)
                wide = adj_buf[:, 2 * TILE * q : 2 * TILE * (q + 1), lanes].astype(jnp.float32)
                if h == 0:
                    cur[y, 2 * q * parts + k] = wide[:, :TILE]
                    cur[y, (2 * q + 1) * parts + k] = wide[:, TILE:]
                else:
                    stage[2 * q * parts + k] = wide[:, :TILE]
                    stage[(2 * q + 1) * parts + k] = wide[:, TILE:]
    dep_copy.wait()
    landing(y)

    @pl.when(jnp.logical_not(has_lower))
    def _():
        rx_lo[...] = jnp.zeros_like(rx_lo)

    @pl.when(jnp.logical_not(has_upper))
    def _():
        rx_hi[...] = jnp.zeros_like(rx_hi)


    peers = sum(
        jnp.where(there, 1, 0)
        for there in (slabs > 1, has_lower, has_upper, p >= 1, p + 1 < pencils)
    )
    pl.semaphore_wait(barrier, peers)

    def feed(k):
        for u in range(1, steps):
            c = k - offsets[u]

            @pl.when(jnp.logical_and(c >= 0, c < chunks))
            def _():
                frac_copy(u, c).start()

        @pl.when(k < chunks)
        def _():
            cur_copy(k).start()
            frac_copy(0, k).start()

        return 0

    land_copy(y).start()
    feed(jnp.int32(0))

    @pl.when(sends_relay)
    def _():
        relay_copy.start()

    lax.fori_loop(1, AHEAD, lambda k, z: feed(k), 0)
    for send, _, copy in halos:
        @pl.when(send)
        def _():
            copy.start()

    for u in range(steps):
        own_copy(u).wait()
    land_copy(other).wait_recv()

    target = lax.broadcasted_iota(jnp.int32, (hot_rows, 4 * rows * TILE), 0)

    def build(u, c):
        tile = lax.div(c, parts)

        @pl.when(lax.rem(c, parts) == 0)
        def _():
            picks = [target == land_buf[h, tile, pl.ds(steps - 1 - u, 1), :] for h in range(2)]
            picks = [jnp.where(pick, 1.0, 0.0).astype(jnp.bfloat16) for pick in picks]
            hot_buf[tile, u] = jnp.concatenate(picks, axis=1)

    def weights(u, c, piece=whole[0]):
        tables = []
        for h in range(2):
            f = frac_buf[(h, u, slice(None)) + place(c, 0, piece)]
            square = f * f
            rest = 1.0 - f
            w0 = rest * rest * (rest * (1.0 / 6.0))
            w1 = square * (0.5 * f - 1.0) + (2.0 / 3.0)
            w3 = square * (f * (1.0 / 6.0))
            tables.append((w0, w1, ((1.0 - w0) - w3) - w1, w3))
        return tables

    def splat(u, c, tables, values, piece=whole[0]):
        _, skip, wide = piece
        hot = hot_buf[lax.div(c, parts), u]
        products = [
            (w * v).reshape(rows * TILE, wide) for table, v in zip(tables, values) for w in table
        ]
        high = [part.astype(jnp.bfloat16) for part in products]
        low = [(a - b.astype(jnp.float32)).astype(jnp.bfloat16) for a, b in zip(products, high)]
        out = jnp.dot(
            jnp.concatenate([hot, hot], axis=1),
            jnp.concatenate(high + low, axis=0),
            preferred_element_type=jnp.float32,
        )
        out = out[: span * TILE].reshape(span, TILE, wide)
        lanes = pl.ds(skip, wide)
        tx_up[u, c, :, :, lanes] = out[BELOW + tall :]
        tx_dn[u, c, :, :, lanes] = out[:BELOW]

        @pl.when(has_upper)
        def _():
            up_copy(u, c, piece).start()

        @pl.when(has_lower)
        def _():
            dn_copy(u, c, piece).start()

        acc[c, :, :, lanes] = out[BELOW : BELOW + tall]

    def arrive(u, c, piece=whole[0]):
        @pl.when(has_lower)
        def _():
            up_copy(u, c, piece).wait_recv()

        @pl.when(has_upper)
        def _():
            dn_copy(u, c, piece).wait_recv()

    def combined(u, c, piece=whole[0]):
        lanes = pl.ds(piece[1], piece[2])
        own = acc[c, :, :, lanes]
        low = rx_lo[u, c, :, :, lanes]
        high = rx_hi[u, c, :, :, lanes]
        top = tall - BELOW
        sums = []
        for r in range(tall):
            total = own[r]
            if r < ABOVE:
                total = total + low[r]
            if r >= top:
                total = total + high[r - top]
            sums.append(total.astype(jnp.bfloat16).astype(jnp.float32))
        return sums

    def halves(c, u, piece=whole[0]):
        total = combined(u, c, piece)
        return jnp.stack(total[:rows]), jnp.stack(total[rows:])

    def start_splat(c):
        build(0, c)
        cur_copy(c).wait_recv()
        frac_copy(0, c).wait_recv()
        splat(0, c, weights(0, c), (cur[0, c], cur[1, c]))

    def finish(c, piece=whole[0]):
        lanes = pl.ds(piece[1], piece[2])
        arrive(steps - 1, c, piece)
        acc[c, :, :, lanes] = jnp.stack(combined(steps - 1, c, piece))
        back_copy(c, piece).start()
        adj_out[(slice(None),) + place(c, y * half, piece)] = acc[c, pl.ds(y * rows, rows), :, lanes]

    def advance(u, c):
        build(u, c)
        frac_copy(u, c).wait_recv()
        tables = weights(u, c)
        arrive(u - 1, c)
        splat(u, c, tables, halves(c, u - 1))

    grad_lane = lax.broadcasted_iota(jnp.int32, (cols, line), 1)

    def across(r):
        grad_out[0, r] = (img_pad[r + 2, TILE : TILE + cols] - img_pad[r, TILE : TILE + cols]) * 0.5

    def gradient(r):
        @pl.when(jnp.logical_and(r >= 1, r < rows - 1))
        def _():
            across(r)

        grad_out[1, r] = (
            img_pad[r + 1, TILE + 1 : TILE + cols + 1] - img_pad[r + 1, TILE - 1 : TILE + cols - 1]
        ) * 0.5
        center = img_pad[r + 1, TILE : TILE + cols]
        after = jnp.where(grad_lane == line - 1, 0.0, pltpu.roll(center, line - 1, 1))
        before = jnp.where(grad_lane == 0, 0.0, pltpu.roll(center, 1, 1))
        grad_out[2, r] = (after - before) * 0.5

    def borders():
        image_copy.wait()
        for index, (_, receive, copy) in enumerate(halos):
            edge = 0 if index == 0 else cols + TILE

            @pl.when(receive)
            def _():
                copy.wait_recv()

            @pl.when(jnp.logical_not(receive))
            def _():
                img_pad[1 : rows + 1, edge : edge + TILE] = jnp.zeros((rows, TILE, line), jnp.float32)

    def slot(k, z):
        feed(k + AHEAD)

        since = k - IMAGE_SLOT
        q = lax.div(since, IMAGE_GAP)
        turn = jnp.logical_and(since >= 0, lax.rem(since, IMAGE_GAP) == 0)

        @pl.when(jnp.logical_and(turn, q < tiles))
        def _():
            inner_copy(q).start()

            @pl.when(jnp.logical_and(gets_relay, q == 0))
            def _():
                relay_copy.wait_recv()

            @pl.when(gets_relay)
            def _():
                outer_copy(q).start()

        for u in range(1, steps):
            c = k - offsets[u]

            @pl.when(jnp.logical_and(c >= 0, c < chunks))
            def _():
                advance(u, c)

        @pl.when(k < chunks)
        def _():
            start_splat(k)

        @pl.when(k >= offsets[steps])
        def _():
            finish(k - offsets[steps])

        row = k - GRADIENT_SLOT

        @pl.when(row == 0)
        def _():
            borders()

        @pl.when(jnp.logical_and(row >= 0, row < rows))
        def _():
            gradient(row)

        return z

    feed(jnp.int32(AHEAD))
    start_splat(jnp.int32(0))
    lax.fori_loop(1, last_slot, slot, 0)

    final = jnp.int32(chunks - 1)
    if last_slot >= offsets[steps]:
        finish(jnp.int32(last_slot - offsets[steps]))
    build(steps - 1, final)
    frac_copy(steps - 1, final).wait_recv()
    arrive(steps - 2, final)
    for piece in split:
        splat(steps - 1, final, weights(steps - 1, final, piece), halves(final, steps - 2, piece), piece)

    begin = last_slot + 1 - offsets[steps]

    def tail(c, z):
        finish(c)

        return z

    lax.fori_loop(begin, chunks - 1, tail, 0)
    for piece in split:
        finish(final, piece)

    for q in range(tiles):
        inner_copy(q).wait_recv()

        @pl.when(gets_outer)
        def _():
            outer_copy(q).wait_recv()

    @pl.when(jnp.logical_not(gets_outer))
    def _():
        img_pad[y * (rows + 1), TILE : TILE + cols] = jnp.zeros((cols, line), jnp.float32)

    across(0)
    across(rows - 1)

    mine_half = pl.ds(pl.multiple_of(y * half, half), half)
    other_half = pl.ds(pl.multiple_of(other * half, half), half)
    land_copy(y).wait_send()
    remote(stage, cur.at[0], cur_send, cur_recv.at[0, 0], {"slab": partner}).wait_send()
    remote(
        frac_ref.at[:, :, :, other_half], frac_buf.at[0], frac_send, frac_recv.at[0, 0, 0], {"slab": partner}
    ).wait_send()

    @pl.when(has_upper)
    def _():
        remote(tx_up, rx_lo, up_send, up_recv.at[0, 0, 0], {"slab": s + 2}).wait_send()

    @pl.when(has_lower)
    def _():
        remote(tx_dn, rx_hi, dn_send, dn_recv.at[0, 0, 0], {"slab": s - 2}).wait_send()

    for q in range(tiles):
        inner_copy(q).wait_send()

        @pl.when(gets_relay)
        def _():
            outer_copy(q).wait_send()

    @pl.when(sends_relay)
    def _():
        relay_copy.wait_send()

    for send, _, copy in halos:
        @pl.when(send)
        def _():
            copy.wait_send()

    back_all = remote(
        adj_out.at[:, :, mine_half], adj_out.at[:, :, other_half], back_send, back_recv, {"slab": partner}
    )
    back_all.wait_recv()
    back_all.wait_send()


def forces(adj_ref, grad_ref, adj_out, force_out, adj_buf, force_buf, adj_sem, force_sem):
    copies = []
    for r in range(adj_ref.shape[0]):
        mine = adj_ref[r]
        for c in range(3):
            force_buf[c, r] = mine * grad_ref[c, r]
        copies.append(pltpu.make_async_copy(force_buf.at[:, r], force_out.at[:, r], force_sem.at[r]))
        copies[-1].start()
        adj_buf[r] = mine.astype(jnp.bfloat16)
        copies.append(pltpu.make_async_copy(adj_buf.at[r], adj_out.at[r], adj_sem.at[r]))
        copies[-1].start()
    for copy in copies:
        copy.wait()


def shards(slabs, pencils, final_adjoint, departure, fraction, image):
    steps, rows, cols = departure.shape
    line = image.shape[2]
    half = line // 2
    width = WIDTH if half % WIDTH == 0 else half
    tiles = cols // TILE
    chunks = tiles * (half // width)
    tall = 2 * rows
    assert GRADIENT_SLOT + rows <= 3 * chunks
    hot_rows = -(-(BELOW + tall + ABOVE) * TILE // 16) * 16
    assert slabs % 2 == 0 and ABOVE <= tall and cols % (2 * TILE) == 0 and half % 128 == 0

    f32 = jnp.float32
    dma = pltpu.SemaphoreType.DMA
    vmem = pl.BlockSpec(memory_space=pltpu.VMEM)
    hbm = pl.BlockSpec(memory_space=pltpu.HBM)
    adjoint, gradient = pl.pallas_call(
        functools.partial(kernel, slabs, pencils),
        name="splat",
        out_shape=(
            jax.ShapeDtypeStruct((rows, cols, line), f32),
            jax.ShapeDtypeStruct((3, rows, cols, line), f32),
        ),
        in_specs=[hbm, hbm, hbm, hbm],
        out_specs=(vmem, vmem),
        scratch_shapes=[
            pltpu.VMEM((steps, rows, cols), jnp.int32),
            pltpu.VMEM((2, tiles, steps, 4 * rows * TILE), jnp.int32),
            pltpu.VMEM((rows, cols, line), jnp.bfloat16),
            pltpu.VMEM((chunks, rows, TILE, width), f32),
            pltpu.VMEM((2, chunks, rows, TILE, width), f32),
            pltpu.VMEM((2, steps, rows, cols, half), f32),
            pltpu.VMEM((tiles, steps, hot_rows, 8 * rows * TILE), jnp.bfloat16),
            pltpu.VMEM((chunks, tall, TILE, width), f32),
            pltpu.VMEM((steps, chunks, ABOVE, TILE, width), f32),
            pltpu.VMEM((steps, chunks, BELOW, TILE, width), f32),
            pltpu.VMEM((steps, chunks, ABOVE, TILE, width), f32),
            pltpu.VMEM((steps, chunks, BELOW, TILE, width), f32),
            pltpu.VMEM((rows + 2, cols + 2 * TILE, line), f32),
            pltpu.VMEM((1, cols, line), f32),
            dma(()),
            dma((2,)),
            dma(()),
            dma(()),
            dma((chunks, 2)),
            dma((steps,)),
            dma(()),
            dma((steps, chunks, 2)),
            dma(()),
            dma((steps, chunks, 2)),
            dma(()),
            dma((steps, chunks, 2)),
            dma(()),
            dma(()),
            dma(()),
            dma((2, 3)),
            dma((2, tiles)),
            dma((2, tiles)),
        ],
        compiler_params=pltpu.CompilerParams(
            collective_id=0, has_side_effects=True, vmem_limit_bytes=40 * 1024 * 1024
        ),
    )(*(pltpu.with_memory_space_constraint(a, pltpu.HBM) for a in (departure, final_adjoint, fraction, image)))
    return pl.pallas_call(
        forces,
        name="forces",
        out_shape=(
            jax.ShapeDtypeStruct((rows, cols, line), jnp.bfloat16),
            jax.ShapeDtypeStruct((3, rows, cols, line), f32),
        ),
        in_specs=[vmem, vmem],
        out_specs=(hbm, hbm),
        scratch_shapes=[
            pltpu.VMEM((rows, cols, line), jnp.bfloat16),
            pltpu.VMEM((3, rows, cols, line), f32),
            dma((rows,)),
            dma((rows,)),
        ],
        compiler_params=pltpu.CompilerParams(vmem_limit_bytes=16 * 1024 * 1024),
    )(adjoint, gradient)


def solution(mesh):
    in_specs = (
        P("slab", "pencil", None),
        P(None, "slab", "pencil"),
        P(None, "slab", "pencil", None),
        P("slab", "pencil", None),
    )
    out_specs = (P("slab", "pencil", None), P(None, "slab", "pencil", None))
    body = functools.partial(shards, mesh.shape["slab"], mesh.shape["pencil"])
    return jax.shard_map(body, mesh=mesh, in_specs=in_specs, out_specs=out_specs, check_vma=False)
```

```python
import functools

import jax
import jax.numpy as jnp
from jax import lax
from jax.experimental import pallas as pl
from jax.experimental.pallas import tpu as pltpu
from jax.sharding import PartitionSpec as P

BELOW = 5
ABOVE = 6
TILE = 8
WIDTH = 256
OFFSETS = (0, 3, 8, 13, 19)
AHEAD = 9
IMAGE_SLOT = 12
IMAGE_GAP = 1
SPLIT = True
GRADIENT_SLOT = 2
MESH = pl.DeviceIdType.MESH


def kernel(
    slabs,
    pencils,
    dep_ref,
    adj_ref,
    frac_ref,
    img_ref,
    adj_out,
    grad_out,
    dep_buf,
    land_buf,
    adj_buf,
    stage,
    cur,
    frac_buf,
    hot_buf,
    acc,
    tx_up,
    tx_dn,
    rx_lo,
    rx_hi,
    img_pad,
    relay_buf,
    dep_sem,
    land_sem,
    adj_sem,
    cur_send,
    cur_recv,
    own_sem,
    frac_send,
    frac_recv,
    up_send,
    up_recv,
    dn_send,
    dn_recv,
    back_send,
    back_recv,
    img_sem,
    halo_sem,
    inner_sem,
    outer_sem,
):
    s = lax.axis_index("slab")
    p = lax.axis_index("pencil")
    y = lax.rem(s, 2)
    other = 1 - y
    partner = s + 1 - 2 * y
    pair = lax.div(s, 2)
    has_lower = s >= 2
    has_upper = s + 2 < slabs

    rows, cols, line = adj_out.shape
    half = line // 2
    width = stage.shape[-1]
    hot_rows = hot_buf.shape[2]
    parts = half // width
    tiles = cols // TILE
    chunks = tiles * parts
    steps = frac_ref.shape[0]
    tall = 2 * rows
    span = BELOW + tall + ABOVE
    offsets = OFFSETS if steps == 4 and chunks == 8 else tuple(u * chunks for u in range(steps + 1))
    last_slot = chunks - 1 + offsets[steps - 1]
    whole = ((0, 0, width),)
    split = ((0, 0, width // 2), (1, width // 2, width // 2)) if SPLIT and width % 256 == 0 else whole

    def remote(src, dst, send_sem, recv_sem, where):
        return pltpu.make_async_remote_copy(
            src_ref=src,
            dst_ref=dst,
            send_sem=send_sem,
            recv_sem=recv_sem,
            device_id=where,
            device_id_type=MESH,
        )

    def place(c, start, piece=whole[0]):
        _, skip, wide = piece
        first = pl.multiple_of(lax.div(c, parts) * TILE, TILE)
        lanes = pl.multiple_of(start + lax.rem(c, parts) * width + skip, wide)
        return pl.ds(first, TILE), pl.ds(lanes, wide)

    def cut(ref, at, piece):
        return ref.at[at + (slice(None), slice(None), pl.ds(piece[1], piece[2]))]

    def own_copy(u):
        return pltpu.make_async_copy(
            frac_ref.at[steps - 1 - u, :, :, pl.ds(pl.multiple_of(y * half, half), half)],
            frac_buf.at[y, u],
            own_sem.at[u],
        )

    def frac_copy(u, c, piece=whole[0]):
        return remote(
            frac_ref.at[(steps - 1 - u, slice(None)) + place(c, other * half, piece)],
            frac_buf.at[(y, u, slice(None)) + place(c, 0, piece)],
            frac_send,
            frac_recv.at[u, c, piece[0]],
            {"slab": partner},
        )

    def cur_copy(c, piece=whole[0]):
        return remote(
            cut(stage, (c,), piece), cut(cur, (y, c), piece), cur_send, cur_recv.at[c, piece[0]], {"slab": partner}
        )

    def land_copy(h):
        return remote(land_buf.at[h], land_buf.at[h], land_sem.at[0], land_sem.at[1], {"slab": partner})

    def up_copy(u, c, piece=whole[0]):
        return remote(
            cut(tx_up, (u, c), piece), cut(rx_lo, (u, c), piece), up_send, up_recv.at[u, c, piece[0]], {"slab": s + 2}
        )

    def dn_copy(u, c, piece=whole[0]):
        return remote(
            cut(tx_dn, (u, c), piece), cut(rx_hi, (u, c), piece), dn_send, dn_recv.at[u, c, piece[0]], {"slab": s - 2}
        )

    def back_copy(c, piece=whole[0]):
        return remote(
            acc.at[c, pl.ds(other * rows, rows), :, pl.ds(piece[1], piece[2])],
            adj_out.at[(slice(None),) + place(c, y * half, piece)],
            back_send,
            back_recv,
            {"slab": partner},
        )

    center_cols = pl.ds(TILE, cols)
    image_copy = pltpu.make_async_copy(
        img_ref, img_pad.at[pl.ds(1, rows), center_cols], img_sem
    )
    relay_to = s + 4 * y - 2
    relay_from = s + 2 - 4 * y
    outer = s + 2 * y - 1
    sends_relay = jnp.logical_and(relay_to >= 0, relay_to < slabs)
    gets_relay = jnp.logical_and(relay_from >= 0, relay_from < slabs)
    gets_outer = jnp.logical_and(outer >= 0, outer < slabs)

    def halo(src, dst, index, where):
        return remote(src, dst, halo_sem.at[0, index], halo_sem.at[1, index], where)

    relay_copy = halo(img_ref.at[pl.ds(y * (rows - 1), 1)], relay_buf, 0, {"slab": relay_to})

    def edge_copy(row, src, src_row, sems, q):
        first = pl.multiple_of(q * TILE, TILE)
        return remote(
            src.at[pl.ds(src_row, 1), pl.ds(first, TILE)],
            img_pad.at[pl.ds(row, 1), pl.ds(pl.multiple_of(first + TILE, TILE), TILE)],
            sems.at[0, q],
            sems.at[1, q],
            {"slab": partner},
        )

    def outer_copy(q):
        return edge_copy(other * (rows + 1), relay_buf, 0, outer_sem, q)

    def inner_copy(q):
        return edge_copy(y * (rows + 1), img_ref, other * (rows - 1), inner_sem, q)

    halos = (
        (p + 1 < pencils, p >= 1, halo(
            img_ref.at[:, pl.ds(cols - TILE, TILE)], img_pad.at[pl.ds(1, rows), pl.ds(0, TILE)],
            1, {"pencil": p + 1})),
        (p >= 1, p + 1 < pencils, halo(
            img_ref.at[:, pl.ds(0, TILE)], img_pad.at[pl.ds(1, rows), pl.ds(cols + TILE, TILE)],
            2, {"pencil": p - 1})),
    )

    barrier = pltpu.get_barrier_semaphore()
    for there, where in (
        (slabs > 1, {"slab": partner}),
        (has_lower, {"slab": s - 2}),
        (has_upper, {"slab": s + 2}),
        (p >= 1, {"pencil": p - 1}),
        (p + 1 < pencils, {"pencil": p + 1}),
    ):
        @pl.when(there)
        def _():
            pl.semaphore_signal(barrier, inc=1, device_id=where, device_id_type=MESH)

    adj_copy = pltpu.make_async_copy(adj_ref, adj_buf, adj_sem)
    dep_copy = pltpu.make_async_copy(dep_ref, dep_buf, dep_sem)
    dep_copy.start()
    adj_copy.start()
    for u in range(steps):
        own_copy(u).start()
    image_copy.start()

    lane = lax.broadcasted_iota(jnp.int32, (steps, 4 * rows * TILE), 1)
    lane_row = lax.rem(lax.div(lane, TILE), rows)
    fixed = lane_row + lax.div(lane, rows * TILE) - 1 + BELOW
    fixed = fixed * TILE + lax.rem(lane, TILE)
    pick_lane = lax.broadcasted_iota(jnp.int32, (cols, 4 * rows * TILE), 1)
    pick_col = lax.broadcasted_iota(jnp.int32, (cols, 4 * rows * TILE), 0)
    keep_lane = lax.broadcasted_iota(jnp.int32, (steps * rows, 4 * rows * TILE), 1)
    keep_row = lax.broadcasted_iota(jnp.int32, (steps * rows, 4 * rows * TILE), 0)
    keep = lax.rem(keep_row, rows) == lax.rem(lax.div(keep_lane, TILE), rows)
    group_step = lax.broadcasted_iota(jnp.int32, (steps, steps * rows), 0)
    group_row = lax.broadcasted_iota(jnp.int32, (steps, steps * rows), 1)
    group = jnp.where(group_step == lax.div(group_row, rows), 1.0, 0.0).astype(jnp.bfloat16)
    row_of = lax.broadcasted_iota(jnp.int32, (rows, cols), 0)

    def landing(h):
        first_row = pair * tall + h * rows
        moved = jnp.concatenate([dep_buf[k] - row_of - first_row for k in range(steps)], axis=0)
        moved = moved.astype(jnp.float32).astype(jnp.bfloat16)
        for tile in range(tiles):
            pick = pick_col == tile * TILE + lax.rem(pick_lane, TILE)
            pick = jnp.where(pick, 1.0, 0.0).astype(jnp.bfloat16)
            spread = jnp.dot(moved, pick, preferred_element_type=jnp.float32)
            spread = jnp.where(keep, spread, 0.0).astype(jnp.bfloat16)
            by_step = jnp.dot(group, spread, preferred_element_type=jnp.float32)
            land_buf[h, tile] = fixed + h * rows * TILE + by_step.astype(jnp.int32) * TILE

    adj_copy.wait()
    for q in range(cols // (2 * TILE)):
        for h in range(2):
            for k in range(parts):
                lanes = pl.ds(pl.multiple_of((y if h == 0 else other) * half + width * k, width), width)
                wide = adj_buf[:, 2 * TILE * q : 2 * TILE * (q + 1), lanes].astype(jnp.float32)
                if h == 0:
                    cur[y, 2 * q * parts + k] = wide[:, :TILE]
                    cur[y, (2 * q + 1) * parts + k] = wide[:, TILE:]
                else:
                    stage[2 * q * parts + k] = wide[:, :TILE]
                    stage[(2 * q + 1) * parts + k] = wide[:, TILE:]
    dep_copy.wait()
    landing(y)

    @pl.when(jnp.logical_not(has_lower))
    def _():
        rx_lo[...] = jnp.zeros_like(rx_lo)

    @pl.when(jnp.logical_not(has_upper))
    def _():
        rx_hi[...] = jnp.zeros_like(rx_hi)


    peers = sum(
        jnp.where(there, 1, 0)
        for there in (slabs > 1, has_lower, has_upper, p >= 1, p + 1 < pencils)
    )
    pl.semaphore_wait(barrier, peers)

    def feed(k):
        for u in range(1, steps):
            c = k - offsets[u]

            @pl.when(jnp.logical_and(c >= 0, c < chunks))
            def _():
                frac_copy(u, c).start()

        @pl.when(k < chunks)
        def _():
            cur_copy(k).start()
            frac_copy(0, k).start()

        return 0

    land_copy(y).start()
    feed(jnp.int32(0))

    @pl.when(sends_relay)
    def _():
        relay_copy.start()

    lax.fori_loop(1, AHEAD, lambda k, z: feed(k), 0)
    for send, _, copy in halos:
        @pl.when(send)
        def _():
            copy.start()

    for u in range(steps):
        own_copy(u).wait()
    land_copy(other).wait_recv()

    target = lax.broadcasted_iota(jnp.int32, (hot_rows, 4 * rows * TILE), 0)

    def build(u, c):
        tile = lax.div(c, parts)

        @pl.when(lax.rem(c, parts) == 0)
        def _():
            picks = [target == land_buf[h, tile, pl.ds(steps - 1 - u, 1), :] for h in range(2)]
            picks = [jnp.where(pick, 1.0, 0.0).astype(jnp.bfloat16) for pick in picks]
            hot_buf[tile, u] = jnp.concatenate(picks, axis=1)

    def weights(u, c, piece=whole[0]):
        tables = []
        for h in range(2):
            f = frac_buf[(h, u, slice(None)) + place(c, 0, piece)]
            square = f * f
            rest = 1.0 - f
            w0 = rest * rest * (rest * (1.0 / 6.0))
            w1 = square * (0.5 * f - 1.0) + (2.0 / 3.0)
            w3 = square * (f * (1.0 / 6.0))
            tables.append((w0, w1, ((1.0 - w0) - w3) - w1, w3))
        return tables

    def splat(u, c, tables, values, piece=whole[0]):
        _, skip, wide = piece
        hot = hot_buf[lax.div(c, parts), u]
        products = [
            (w * v).reshape(rows * TILE, wide) for table, v in zip(tables, values) for w in table
        ]
        high = [part.astype(jnp.bfloat16) for part in products]
        low = [(a - b.astype(jnp.float32)).astype(jnp.bfloat16) for a, b in zip(products, high)]
        out = jnp.dot(
            jnp.concatenate([hot, hot], axis=1),
            jnp.concatenate(high + low, axis=0),
            preferred_element_type=jnp.float32,
        )
        out = out[: span * TILE].reshape(span, TILE, wide)
        lanes = pl.ds(skip, wide)
        tx_up[u, c, :, :, lanes] = out[BELOW + tall :]
        tx_dn[u, c, :, :, lanes] = out[:BELOW]

        @pl.when(has_upper)
        def _():
            up_copy(u, c, piece).start()

        @pl.when(has_lower)
        def _():
            dn_copy(u, c, piece).start()

        acc[c, :, :, lanes] = out[BELOW : BELOW + tall]

    def arrive(u, c, piece=whole[0]):
        @pl.when(has_lower)
        def _():
            up_copy(u, c, piece).wait_recv()

        @pl.when(has_upper)
        def _():
            dn_copy(u, c, piece).wait_recv()

    def combined(u, c, piece=whole[0]):
        lanes = pl.ds(piece[1], piece[2])
        own = acc[c, :, :, lanes]
        low = rx_lo[u, c, :, :, lanes]
        high = rx_hi[u, c, :, :, lanes]
        top = tall - BELOW
        sums = []
        for r in range(tall):
            total = own[r]
            if r < ABOVE:
                total = total + low[r]
            if r >= top:
                total = total + high[r - top]
            sums.append(total.astype(jnp.bfloat16).astype(jnp.float32))
        return sums

    def halves(c, u, piece=whole[0]):
        total = combined(u, c, piece)
        return jnp.stack(total[:rows]), jnp.stack(total[rows:])

    def start_splat(c):
        build(0, c)
        cur_copy(c).wait_recv()
        frac_copy(0, c).wait_recv()
        splat(0, c, weights(0, c), (cur[0, c], cur[1, c]))

    def finish(c, piece=whole[0]):
        lanes = pl.ds(piece[1], piece[2])
        arrive(steps - 1, c, piece)
        acc[c, :, :, lanes] = jnp.stack(combined(steps - 1, c, piece))
        back_copy(c, piece).start()
        adj_out[(slice(None),) + place(c, y * half, piece)] = acc[c, pl.ds(y * rows, rows), :, lanes]

    def advance(u, c):
        build(u, c)
        frac_copy(u, c).wait_recv()
        tables = weights(u, c)
        arrive(u - 1, c)
        splat(u, c, tables, halves(c, u - 1))

    grad_lane = lax.broadcasted_iota(jnp.int32, (cols, line), 1)

    def across(r):
        grad_out[0, r] = (img_pad[r + 2, TILE : TILE + cols] - img_pad[r, TILE : TILE + cols]) * 0.5

    def gradient(r):
        @pl.when(jnp.logical_and(r >= 1, r < rows - 1))
        def _():
            across(r)

        grad_out[1, r] = (
            img_pad[r + 1, TILE + 1 : TILE + cols + 1] - img_pad[r + 1, TILE - 1 : TILE + cols - 1]
        ) * 0.5
        center = img_pad[r + 1, TILE : TILE + cols]
        after = jnp.where(grad_lane == line - 1, 0.0, pltpu.roll(center, line - 1, 1))
        before = jnp.where(grad_lane == 0, 0.0, pltpu.roll(center, 1, 1))
        grad_out[2, r] = (after - before) * 0.5

    def borders():
        image_copy.wait()
        for index, (_, receive, copy) in enumerate(halos):
            edge = 0 if index == 0 else cols + TILE

            @pl.when(receive)
            def _():
                copy.wait_recv()

            @pl.when(jnp.logical_not(receive))
            def _():
                img_pad[1 : rows + 1, edge : edge + TILE] = jnp.zeros((rows, TILE, line), jnp.float32)

    def slot(k, z):
        feed(k + AHEAD)

        since = k - IMAGE_SLOT
        q = lax.div(since, IMAGE_GAP)
        turn = jnp.logical_and(since >= 0, lax.rem(since, IMAGE_GAP) == 0)

        @pl.when(jnp.logical_and(turn, q < tiles))
        def _():
            inner_copy(q).start()

            @pl.when(jnp.logical_and(gets_relay, q == 0))
            def _():
                relay_copy.wait_recv()

            @pl.when(gets_relay)
            def _():
                outer_copy(q).start()

        for u in range(1, steps):
            c = k - offsets[u]

            @pl.when(jnp.logical_and(c >= 0, c < chunks))
            def _():
                advance(u, c)

        @pl.when(k < chunks)
        def _():
            start_splat(k)

        @pl.when(k >= offsets[steps])
        def _():
            finish(k - offsets[steps])

        row = k - GRADIENT_SLOT

        @pl.when(row == 0)
        def _():
            borders()

        @pl.when(jnp.logical_and(row >= 0, row < rows))
        def _():
            gradient(row)

        return z

    feed(jnp.int32(AHEAD))
    start_splat(jnp.int32(0))
    lax.fori_loop(1, last_slot, slot, 0)

    final = jnp.int32(chunks - 1)
    if last_slot >= offsets[steps]:
        finish(jnp.int32(last_slot - offsets[steps]))
    build(steps - 1, final)
    frac_copy(steps - 1, final).wait_recv()
    arrive(steps - 2, final)
    for piece in split:
        splat(steps - 1, final, weights(steps - 1, final, piece), halves(final, steps - 2, piece), piece)

    begin = last_slot + 1 - offsets[steps]

    def tail(c, z):
        finish(c)

        return z

    lax.fori_loop(begin, chunks - 1, tail, 0)
    for piece in split:
        finish(final, piece)

    for q in range(tiles):
        inner_copy(q).wait_recv()

        @pl.when(gets_outer)
        def _():
            outer_copy(q).wait_recv()

    @pl.when(jnp.logical_not(gets_outer))
    def _():
        img_pad[y * (rows + 1), TILE : TILE + cols] = jnp.zeros((cols, line), jnp.float32)

    across(0)
    across(rows - 1)

    mine_half = pl.ds(pl.multiple_of(y * half, half), half)
    other_half = pl.ds(pl.multiple_of(other * half, half), half)
    land_copy(y).wait_send()
    remote(stage, cur.at[0], cur_send, cur_recv.at[0, 0], {"slab": partner}).wait_send()
    remote(
        frac_ref.at[:, :, :, other_half], frac_buf.at[0], frac_send, frac_recv.at[0, 0, 0], {"slab": partner}
    ).wait_send()

    @pl.when(has_upper)
    def _():
        remote(tx_up, rx_lo, up_send, up_recv.at[0, 0, 0], {"slab": s + 2}).wait_send()

    @pl.when(has_lower)
    def _():
        remote(tx_dn, rx_hi, dn_send, dn_recv.at[0, 0, 0], {"slab": s - 2}).wait_send()

    for q in range(tiles):
        inner_copy(q).wait_send()

        @pl.when(gets_relay)
        def _():
            outer_copy(q).wait_send()

    @pl.when(sends_relay)
    def _():
        relay_copy.wait_send()

    for send, _, copy in halos:
        @pl.when(send)
        def _():
            copy.wait_send()

    back_all = remote(
        adj_out.at[:, :, mine_half], adj_out.at[:, :, other_half], back_send, back_recv, {"slab": partner}
    )
    back_all.wait_recv()
    back_all.wait_send()


def forces(adj_ref, grad_ref, adj_out, force_out, adj_buf, force_buf, adj_sem, force_sem):
    copies = []
    for r in range(adj_ref.shape[0]):
        mine = adj_ref[r]
        for c in range(3):
            force_buf[c, r] = mine * grad_ref[c, r]
        copies.append(pltpu.make_async_copy(force_buf.at[:, r], force_out.at[:, r], force_sem.at[r]))
        copies[-1].start()
        adj_buf[r] = mine.astype(jnp.bfloat16)
        copies.append(pltpu.make_async_copy(adj_buf.at[r], adj_out.at[r], adj_sem.at[r]))
        copies[-1].start()
    for copy in copies:
        copy.wait()


def shards(slabs, pencils, final_adjoint, departure, fraction, image):
    steps, rows, cols = departure.shape
    line = image.shape[2]
    half = line // 2
    width = WIDTH if half % WIDTH == 0 else half
    tiles = cols // TILE
    chunks = tiles * (half // width)
    tall = 2 * rows
    assert GRADIENT_SLOT + rows <= 3 * chunks
    hot_rows = -(-(BELOW + tall + ABOVE) * TILE // 16) * 16
    assert slabs % 2 == 0 and ABOVE <= tall and cols % (2 * TILE) == 0 and half % 128 == 0

    f32 = jnp.float32
    dma = pltpu.SemaphoreType.DMA
    vmem = pl.BlockSpec(memory_space=pltpu.VMEM)
    hbm = pl.BlockSpec(memory_space=pltpu.HBM)
    adjoint, gradient = pl.pallas_call(
        functools.partial(kernel, slabs, pencils),
        name="splat",
        out_shape=(
            jax.ShapeDtypeStruct((rows, cols, line), f32),
            jax.ShapeDtypeStruct((3, rows, cols, line), f32),
        ),
        in_specs=[hbm, hbm, hbm, hbm],
        out_specs=(vmem, vmem),
        scratch_shapes=[
            pltpu.VMEM((steps, rows, cols), jnp.int32),
            pltpu.VMEM((2, tiles, steps, 4 * rows * TILE), jnp.int32),
            pltpu.VMEM((rows, cols, line), jnp.bfloat16),
            pltpu.VMEM((chunks, rows, TILE, width), f32),
            pltpu.VMEM((2, chunks, rows, TILE, width), f32),
            pltpu.VMEM((2, steps, rows, cols, half), f32),
            pltpu.VMEM((tiles, steps, hot_rows, 8 * rows * TILE), jnp.bfloat16),
            pltpu.VMEM((chunks, tall, TILE, width), f32),
            pltpu.VMEM((steps, chunks, ABOVE, TILE, width), f32),
            pltpu.VMEM((steps, chunks, BELOW, TILE, width), f32),
            pltpu.VMEM((steps, chunks, ABOVE, TILE, width), f32),
            pltpu.VMEM((steps, chunks, BELOW, TILE, width), f32),
            pltpu.VMEM((rows + 2, cols + 2 * TILE, line), f32),
            pltpu.VMEM((1, cols, line), f32),
            dma(()),
            dma((2,)),
            dma(()),
            dma(()),
            dma((chunks, 2)),
            dma((steps,)),
            dma(()),
            dma((steps, chunks, 2)),
            dma(()),
            dma((steps, chunks, 2)),
            dma(()),
            dma((steps, chunks, 2)),
            dma(()),
            dma(()),
            dma(()),
            dma((2, 3)),
            dma((2, tiles)),
            dma((2, tiles)),
        ],
        compiler_params=pltpu.CompilerParams(
            collective_id=0, has_side_effects=True, vmem_limit_bytes=40 * 1024 * 1024
        ),
    )(*(pltpu.with_memory_space_constraint(a, pltpu.HBM) for a in (departure, final_adjoint, fraction, image)))
    return pl.pallas_call(
        forces,
        name="forces",
        out_shape=(
            jax.ShapeDtypeStruct((rows, cols, line), jnp.bfloat16),
            jax.ShapeDtypeStruct((3, rows, cols, line), f32),
        ),
        in_specs=[vmem, vmem],
        out_specs=(hbm, hbm),
        scratch_shapes=[
            pltpu.VMEM((rows, cols, line), jnp.bfloat16),
            pltpu.VMEM((3, rows, cols, line), f32),
            dma((rows,)),
            dma((rows,)),
        ],
        compiler_params=pltpu.CompilerParams(vmem_limit_bytes=16 * 1024 * 1024),
    )(adjoint, gradient)


def solution(mesh):
    in_specs = (
        P("slab", "pencil", None),
        P(None, "slab", "pencil"),
        P(None, "slab", "pencil", None),
        P("slab", "pencil", None),
    )
    out_specs = (P("slab", "pencil", None), P(None, "slab", "pencil", None))
    body = functools.partial(shards, mesh.shape["slab"], mesh.shape["pencil"])
    return jax.shard_map(body, mesh=mesh, in_specs=in_specs, out_specs=out_specs, check_vma=False)
```
